512 devices in a mesh: leaf: 32 (over y, x), node: 16 (over z, core).
Axes of the slice: x: 4, y: 8, z: 8, core: 2. Of those that a mesh axis runs over, the one named last changes fastest.
Arguments:
- positions: float32 [3, 524288], P(None, ('leaf', 'node')), may hold values from 0 to 64, as said below
- charges: float32 [524288], P(('leaf', 'node')), may hold values from -0.625 to 0.625
- near_list: int32 [1024, 26], P(('leaf', 'node')), may hold values from 0 to 1023, as said below
- near_count: int32 [1024], P(('leaf', 'node')), may hold values from 1 to 26, as said below
- far_sample: float32 [524288, 128], P(('leaf', 'node')), may hold values from -0.625 to 0.625
- proxies: float32 [1024, 3, 128], P(('leaf', 'node')), may hold values from -2 to 66, as said below
- strengths: float32 [1024, 128], P(('leaf', 'node')), may hold values from 0.005 to 0.05
Outputs:
- near_potential: float32 [524288], P(('leaf', 'node'))
- leaf_coeffs: float32 [1024, 128], P(('leaf', 'node'))
- top_factor: float32 [32, 128, 128], P('leaf', 'node')
- top_coeffs: float32 [32, 128], P('leaf', 'node')
The draws below stay inside these ranges and needn't reach their ends.
Inputs may be any that keep to these rules, and one draw needn't show every extreme that they name: `near_list`: each entry of row g is a leaf other than g whose cube touches the cube of leaf g (shares a face, an edge or a corner); the entries before near_count[g] are distinct. `near_count`: slots of a row at or past its count are not used; some leaf uses all 26 slots. `positions`: the particles of leaf g lie in the unit cube whose lowest corner is (g // 16, (g // 4) % 4, g % 4). `proxies`: the proxy points of leaf g lie at distance 1.5 to 2 from the centre of its cube.
All inputs are finite; a program needn't handle non-finite values.
Results may differ from the reference program's by a relative error of at most 0.0003.
Values sent between devices are 32-bit elements; how exact they have to be, the bound alone decides.
A program may use at most 64 MiB of HBM per device.

```python
import math
import jax
import jax.numpy as jnp
import numpy as np
from jax import lax

P_SIZE = 512
R = 128
LEAVES = 1024
PARTICLES = 524288
CROSS_Y = 4
CROSS_Z = 4
SLICES = 64
NEAR = 26
N_LEAF = 32


def near_tables(key):
    key_list = jax.random.split(jax.random.fold_in(key, 7), 4)
    offset_table = jnp.asarray(np.array([[first_step, second_step, third_step] for first_step in (-1, 0, 1) for second_step in (-1, 0, 1) for third_step in (-1, 0, 1) if first_step != 0 or second_step != 0 or third_step != 0], dtype=np.int32))
    across = CROSS_Y * CROSS_Z
    leaf_index = jnp.arange(LEAVES, dtype=jnp.int32)
    slab_index = leaf_index // across
    row_index = leaf_index // CROSS_Z % CROSS_Y
    column_index = leaf_index % CROSS_Z
    slab_next = slab_index[:, None] + offset_table[None, :, 0]
    row_next = row_index[:, None] + offset_table[None, :, 1]
    column_next = column_index[:, None] + offset_table[None, :, 2]
    inside = (slab_next >= 0) & (slab_next < SLICES) & (row_next >= 0) & (row_next < CROSS_Y) & (column_next >= 0) & (column_next < CROSS_Z)
    target = slab_next * across + row_next * CROSS_Z + column_next
    scores = jax.random.randint(key_list[0], (LEAVES, 26), 0, 1 << 16) * 64 + jnp.arange(26, dtype=jnp.int32)[None, :]
    scores = scores + jnp.where(inside, 0, 1 << 23)
    order = jnp.argsort(scores, axis=1)[:, :NEAR]
    chosen = jnp.take_along_axis(target, order, axis=1)
    available = jnp.sum(inside.astype(jnp.int32), 1)
    slot_index = jnp.arange(NEAR, dtype=jnp.int32)[None, :]
    chosen = jnp.where(slot_index < available[:, None], chosen, chosen[:, :1])
    dense = jax.random.randint(key_list[1], (LEAVES,), 0, 4) == 0
    forced_slab = jax.random.randint(key_list[2], (), 1, SLICES - 1)
    forced = forced_slab * across + min(1, CROSS_Y - 1) * CROSS_Z + min(1, CROSS_Z - 1)
    dense = dense | (leaf_index == forced)
    sparse = jax.random.randint(key_list[3], (LEAVES,), 1, max(NEAR // 4, 1) + 1)
    counts = jnp.where(dense, available, jnp.minimum(sparse, available))
    return (chosen.astype(jnp.int32), counts.astype(jnp.int32))


def draw_near_list(key, part):
    return near_tables(key)[0]


def draw_near_count(key, part):
    return near_tables(key)[1]


def leaf_corner(leaf_index):
    slab_index = leaf_index // (CROSS_Y * CROSS_Z)
    row_index = leaf_index // CROSS_Z % CROSS_Y
    column_index = leaf_index % CROSS_Z
    return jnp.stack([slab_index, row_index, column_index]).astype(jnp.float32)


def draw_positions(key, part):
    cube = jax.random.uniform(jax.random.fold_in(key, 11), (3, PARTICLES), jnp.float32)
    leaf_index = jnp.arange(PARTICLES, dtype=jnp.int32) // P_SIZE
    return cube + leaf_corner(leaf_index)


def draw_proxies(key, part):
    key_list = jax.random.split(jax.random.fold_in(key, 13), 3)
    polar = jax.random.uniform(key_list[0], (LEAVES, R), jnp.float32) * math.pi
    azimuth = jax.random.uniform(key_list[1], (LEAVES, R), jnp.float32) * (2.0 * math.pi)
    radius = jax.random.uniform(key_list[2], (LEAVES, R), jnp.float32, 1.5, 2.0)
    centre = leaf_corner(jnp.arange(LEAVES, dtype=jnp.int32)) + 0.5
    first = centre[0][:, None] + radius * jnp.sin(polar) * jnp.cos(azimuth)
    second = centre[1][:, None] + radius * jnp.sin(polar) * jnp.sin(azimuth)
    third = centre[2][:, None] + radius * jnp.cos(polar)
    return jnp.stack([first, second, third], 1)


def steps_of(key, dims, cuts, smallest, high):
    factor_of = 1.0
    for axis_at, shards_of in cuts:
        heights = jax.random.uniform(jax.random.fold_in(jax.random.fold_in(key, 6), axis_at), (shards_of,), jnp.float32, smallest / len(cuts), high / len(cuts))
        factor_of = factor_of * jnp.repeat(jnp.exp(heights), dims[axis_at] // shards_of).reshape((-1,) + (1,) * (len(dims) - 1 - axis_at))
    return factor_of


def noise(key, dims, deviation, most, pieces=(), held_as=jnp.bfloat16):
    entries = deviation * jax.random.normal(key, dims, jnp.float32)
    if pieces:
        entries = entries * steps_of(key, dims, pieces, -0.22, 0.18)
    return jnp.clip(entries, -most, most).astype(held_as)


def setup_inputs(seed: int = 0) -> dict:
    key_of = jax.random.split(jax.random.key(seed), 8)
    positions = draw_positions(jax.random.fold_in(key_of[7], 71), 0)
    charges = noise(key_of[1], (PARTICLES,), (P_SIZE ** -0.5), 0.625, ((0, 512),), jnp.float32)
    near_list = draw_near_list(jax.random.fold_in(key_of[7], 71), 0)
    near_count = draw_near_count(jax.random.fold_in(key_of[7], 71), 0)
    far_sample = noise(key_of[4], (PARTICLES, R), (P_SIZE ** -0.5), 0.625, ((0, 512),), jnp.float32)
    proxies = draw_proxies(jax.random.fold_in(key_of[7], 71), 0)
    strengths = jnp.clip(jnp.exp(math.log(0.05) - 2.3025851 * jax.random.uniform(key_of[6], (LEAVES, R), jnp.float32) ** steps_of(key_of[6], (LEAVES, R), ((0, 512),), -0.2, 0.2)), 0.005, 0.05)
    return dict(positions=positions, charges=charges, near_list=near_list, near_count=near_count, far_sample=far_sample, proxies=proxies, strengths=strengths)


soft_square = 0.0025

def leaf_basis(points, weights, sample, proxies, strengths):
    highest = lax.Precision.HIGHEST
    square_sum = jnp.zeros(sample.shape, jnp.float32)
    for component in range(3):
        separation = points[:, component, :, None] - proxies[:, component, None, :]
        square_sum = square_sum + separation * separation
    response = sample + lax.rsqrt(square_sum + soft_square) * strengths[:, None, :]
    gram_matrix = jnp.einsum('npr,nps->nrs', response, response, precision=highest)
    moment = jnp.einsum('npr,np->nr', response, weights, precision=highest)
    factor = jnp.linalg.cholesky(gram_matrix)
    coeffs = lax.linalg.triangular_solve(factor, moment[..., None], left_side=True, lower=True)[..., 0]
    return (factor, coeffs)

def merge_pair(left_factor, left_coeffs, right_factor, right_coeffs):
    highest = lax.Precision.HIGHEST
    gram_matrix = jnp.matmul(left_factor, jnp.swapaxes(left_factor, -1, -2), precision=highest)
    gram_matrix = gram_matrix + jnp.matmul(right_factor, jnp.swapaxes(right_factor, -1, -2), precision=highest)
    factor = jnp.linalg.cholesky(gram_matrix)
    moment = jnp.matmul(left_factor, left_coeffs[..., None], precision=highest)
    moment = moment + jnp.matmul(right_factor, right_coeffs[..., None], precision=highest)
    coeffs = lax.linalg.triangular_solve(factor, moment, left_side=True, lower=True)[..., 0]
    return (factor, coeffs)

def tile_sum(target, source):
    square_sum = jnp.zeros((target.shape[1], source.shape[1]), jnp.float32)
    for component in range(3):
        separation = target[component][:, None] - source[component][None, :]
        square_sum = square_sum + separation * separation
    return jnp.dot(lax.rsqrt(square_sum + soft_square), source[3], precision=lax.Precision.HIGHEST)

def reference(positions, charges, near_list, near_count, far_sample, proxies, strengths):
    points = positions.reshape(3, LEAVES, P_SIZE).transpose(1, 0, 2)
    weights = charges.reshape(LEAVES, P_SIZE)
    samples = far_sample.reshape(LEAVES, P_SIZE, R)

    def one_basis(item):
        point_one, weight_one, sample_one, proxy_one, strength_one = item
        factor, coeffs = leaf_basis(point_one[None], weight_one[None], sample_one[None], proxy_one[None], strength_one[None])
        return (factor[0], coeffs[0])
    factor, coeffs = lax.map(one_basis, (points, weights, samples, proxies, strengths))
    leaf_coeffs = coeffs
    while factor.shape[0] > N_LEAF:
        factor, coeffs = merge_pair(factor[0::2], coeffs[0::2], factor[1::2], coeffs[1::2])
    packed = jnp.concatenate([points, weights[:, None, :]], 1)

    def one_leaf(member):
        own_points = packed[member]
        sources = packed[near_list[member]]
        terms = jax.vmap(tile_sum, in_axes=(None, 0))(own_points, sources)
        live = (jnp.arange(NEAR) < near_count[member]).astype(jnp.float32)
        return tile_sum(own_points, own_points) + lax.optimization_barrier(jnp.sum(terms * live[:, None], 0))
    near_potential = lax.map(one_leaf, jnp.arange(LEAVES, dtype=jnp.int32))
    return (near_potential.reshape(-1), leaf_coeffs, factor, coeffs)
```

```python
import functools

import jax
import jax.numpy as jnp
from jax import lax
from jax.experimental import pallas as pl
from jax.experimental.pallas import tpu as pltpu
from jax.sharding import PartitionSpec as P

soft_square = 0.0025
ACROSS = 4
PANEL = 16
CHUNK = 128
MESH = pl.DeviceIdType.MESH
HIGHEST = lax.Precision.HIGHEST


def split3(v):
    high = v.astype(jnp.bfloat16).astype(jnp.float32)
    rest = v - high
    mid = rest.astype(jnp.bfloat16).astype(jnp.float32)
    return high, mid, rest - mid


def feature_rows(xyz, fourth, fifth):
    row = lax.broadcasted_iota(jnp.int32, (8, xyz.shape[1]), 0)
    rows = jnp.where(row == 4, fifth, 0.0)
    rows = jnp.where(row == 3, fourth, rows)
    for k in range(3):
        rows = jnp.where(row == k, xyz[k : k + 1], rows)
    return split3(rows)


def source_features(xyz):
    high, mid, low = feature_rows(xyz, jnp.sum(xyz * xyz, 0, keepdims=True), 1.0)
    return jnp.concatenate([high, high, high, mid, mid, mid, low, low], 0).astype(jnp.bfloat16)


def target_features(xyz):
    norm = jnp.sum(xyz * xyz, 0, keepdims=True) + soft_square
    high, mid, low = feature_rows(-2.0 * xyz, 1.0, norm)
    return jnp.concatenate([high, mid, low, high, mid, low, high, mid], 0).T.astype(jnp.bfloat16)


def place(node):
    return node // 8, lax.rem(node // 2, ACROSS), lax.rem(node, 2)


def centre_of(block, node):
    slab, y, half = place(node)
    return (
        (2 * block + slab).astype(jnp.float32) + 0.5,
        y.astype(jnp.float32) + 0.5,
        (2 * half).astype(jnp.float32) + 1.0,
    )


def centred(rows, centre):
    row = lax.broadcasted_iota(jnp.int32, rows.shape, 0)
    shift = jnp.where(row == 0, centre[0], jnp.where(row == 1, centre[1], centre[2]))
    return rows - shift


def exchange_kernel(
    blocks,
    nodes,
    pos_ref,
    charge_ref,
    far_ref,
    proxy_ref,
    strength_ref,
    win_ref,
    gram_ref,
    moment_ref,
    top_gram_ref,
    top_moment_ref,
    share,
    parts,
    win_send,
    win_recv,
    rs_send,
    rs_recv,
    ag_send,
    ag_recv,
):
    block = lax.axis_index("leaf")
    node = lax.axis_index("node")
    slab, y, half = place(node)
    size = pos_ref.shape[1] // 2
    rank = far_ref.shape[1]

    def spatial(ds, dy, core):
        level = slab + ds
        step = (level + 2) // 2 - 1
        level = level - 2 * step
        other = level * 8 + lax.rem(y + dy + ACROSS, ACROSS) * 2 + core
        return (lax.rem(block + step + blocks, blocks), other)

    def in_block(k):
        return (block, lax.rem(node + k, nodes))

    outside = 1 - 2 * slab
    barrier = pltpu.get_barrier_semaphore()
    for k in range(1, nodes):
        pl.semaphore_signal(barrier, inc=1, device_id=in_block(k), device_id_type=MESH)
    for dy in (-1, 0, 1):
        for core in (0, 1):
            target = spatial(-outside, dy, core)
            pl.semaphore_signal(barrier, inc=1, device_id=target, device_id_type=MESH)

    for t in range(2):
        lanes = slice(t * size, (t + 1) * size)
        win_ref[4, t, 0:3, :] = pos_ref[:, lanes]
        win_ref[4, t, 3:4, :] = charge_ref[:, lanes]
    centre = centre_of(block, node)
    for t in range(2):
        lanes = slice(t * size, (t + 1) * size)
        distance = jnp.dot(
            target_features(centred(pos_ref[:, lanes], centre)),
            source_features(centred(proxy_ref[t], centre)),
            preferred_element_type=jnp.float32,
        )
        response = far_ref[lanes, :] + lax.rsqrt(distance) * strength_ref[t : t + 1, :]
        gram = lax.dot_general(
            response,
            response,
            (((0,), (0,)), ((), ())),
            precision=HIGHEST,
            preferred_element_type=jnp.float32,
        )
        moment = jnp.dot(
            jnp.broadcast_to(charge_ref[:, lanes], (8, size)),
            response,
            precision=HIGHEST,
            preferred_element_type=jnp.float32,
        )
        gram_ref[t] = gram
        moment_ref[t] = moment
    total = gram_ref[0] + gram_ref[1]
    total_moment = moment_ref[0, 0:1, :] + moment_ref[1, 0:1, :]
    rows = rank // nodes
    for n in range(nodes):
        share[n, 0:rows, :] = total[n * rows : (n + 1) * rows]
        share[n, rows : rows + 1, :] = total_moment

    pl.semaphore_wait(barrier, nodes - 1 + 6)

    rs = []
    for k in range(1, nodes):
        target = in_block(k)
        rs.append(
            pltpu.make_async_remote_copy(
                src_ref=share.at[target[1]],
                dst_ref=parts.at[node],
                send_sem=rs_send.at[k],
                recv_sem=rs_recv.at[k],
                device_id=target,
                device_id_type=MESH,
            )
        )
        rs[-1].start()
    window = []
    for ds in (-1, 0, 1):
        for dy in (-1, 0, 1):
            slot = 4 + 3 * ds + dy
            if slot != 4:
                window.append(
                    pltpu.make_async_remote_copy(
                        src_ref=win_ref.at[4, pl.ds(0, 2)],
                        dst_ref=win_ref.at[8 - slot, pl.ds(0, 2)],
                        send_sem=win_send.at[slot],
                        recv_sem=win_recv.at[slot],
                        device_id=spatial(ds, dy, half),
                        device_id_type=MESH,
                    )
                )
                window[-1].start()
            window.append(
                pltpu.make_async_remote_copy(
                    src_ref=win_ref.at[4, pl.ds(1 - half, 1)],
                    dst_ref=win_ref.at[8 - slot, pl.ds(2, 1)],
                    send_sem=win_send.at[9 + slot],
                    recv_sem=win_recv.at[9 + slot],
                    device_id=spatial(ds, dy, 1 - half),
                    device_id_type=MESH,
                )
            )
            window[-1].start()

    parts[node] = share[node]
    for copy in rs:
        copy.wait_recv()
    sums = parts[0]
    for n in range(1, nodes):
        sums = sums + parts[n]
    top_gram_ref[node] = sums[0:rows]
    top_moment_ref[...] = sums[rows : rows + 1]
    ag = []
    for k in range(1, nodes):
        ag.append(
            pltpu.make_async_remote_copy(
                src_ref=top_gram_ref.at[node],
                dst_ref=top_gram_ref.at[node],
                send_sem=ag_send.at[k],
                recv_sem=ag_recv.at[k],
                device_id=in_block(k),
                device_id_type=MESH,
            )
        )
        ag[-1].start()
    for copy in rs:
        copy.wait_send()
    for copy in window + ag:
        copy.wait()


def leaf_kernel(
    count_ref,
    near_ref,
    win_ref,
    gram_ref,
    moment_ref,
    top_gram_ref,
    top_moment_ref,
    near_out,
    coeffs_out,
    factor_out,
    top_coeffs_out,
    targets,
    weights,
    totals,
    work,
    upper,
):
    block = lax.axis_index("leaf")
    node = lax.axis_index("node")
    slab, y, half = place(node)
    size = win_ref.shape[3]
    rank = gram_ref.shape[1]
    centre = centre_of(block, node)

    row = lax.broadcasted_iota(jnp.int32, (32, near_ref.shape[1]), 0)
    lane = lax.broadcasted_iota(jnp.int32, (32, near_ref.shape[1]), 1)
    ids = jnp.full(row.shape, -1, jnp.int32)
    for k in range(27):
        ds, dy, w = k // 9 - 1, k // 3 % 3 - 1, k % 3
        z = 2 * half + w if w < 2 else 2 - half
        base = (2 * block + slab + ds) * ACROSS * ACROSS
        leaf = base + lax.rem(y + dy + ACROSS, ACROSS) * ACROSS + z
        ids = jnp.where(row == k, leaf, ids)
    for t in range(2):
        hit = (near_ref[t : t + 1, :] == ids) & (lane < count_ref[t])
        weight = jnp.sum(hit.astype(jnp.float32), 1, keepdims=True)
        own = row[:, 0:1] == 12 + t
        weights[t] = jnp.broadcast_to(jnp.where(own, 1.0, weight), (32, 128))
        targets[t] = target_features(centred(win_ref[4, t, 0:3, :], centre))
    totals[...] = jnp.zeros_like(totals)

    def add_tile(t, features, charges, source):
        weight = weights[t, pl.ds(source, 1), :]
        charges = charges * jnp.concatenate([weight] * (size // 128), 1)
        for c in range(size // CHUNK):
            chunk = slice(c * CHUNK, (c + 1) * CHUNK)
            distance = jnp.dot(targets[t, chunk, :], features, preferred_element_type=jnp.float32)
            terms = lax.rsqrt(distance) * charges
            total = terms[:, 0:128]
            for k in range(1, size // 128):
                total = total + terms[:, k * 128 : (k + 1) * 128]
            totals[t, chunk, :] += total

    @pl.loop(0, 9)
    def _(slot):
        for w in range(3):
            points = win_ref[slot, w]
            features = source_features(centred(points[0:3], centre))
            for t in (0, 1) if w < 2 else (1 - half,):
                add_tile(t, features, points[3:4], slot * 3 + w)

    for t in range(2):
        near = lax.dot_general(
            jnp.ones((8, 128), jnp.float32),
            totals[t],
            (((1,), (1,)), ((), ())),
            precision=HIGHEST,
            preferred_element_type=jnp.float32,
        )
        near_out[:, t * size : (t + 1) * size] = near[0:1]

    for i in range(3):
        if i < 2:
            work[i, :, 0:rank] = gram_ref[i]
            moment = moment_ref[i, 0:1, :]
        else:
            work[i, :, 0:rank] = top_gram_ref[...].reshape(rank, rank)
            moment = top_moment_ref[...]
        work[i, :, rank:] = jnp.broadcast_to(moment, (rank, rank)).T
    row = lax.broadcasted_iota(jnp.int32, (PANEL, rank), 0)
    col = lax.broadcasted_iota(jnp.int32, (PANEL, rank), 1)
    for low in range(0, rank, PANEL):
        high = low + PANEL
        for i in range(3):
            panel = work[i, low:high, 0:rank]
            right = work[i, low:high, rank:]
            columns = [
                jnp.broadcast_to(panel[:, low + j : low + j + 1], (PANEL, rank))
                for j in range(PANEL)
            ]
            done = jnp.zeros((PANEL, rank), jnp.float32)
            done_right = done
            for j in range(PANEL):
                inverse = lax.rsqrt(columns[j][j : j + 1, :])
                below = jnp.where(row > j, columns[j] * inverse, 0.0)
                pivot = panel[j : j + 1] * inverse
                pivot_right = right[j : j + 1] * inverse
                done = jnp.where(row == j, pivot, done)
                done_right = jnp.where(row == j, pivot_right, done_right)
                if j + 1 < PANEL:
                    panel = panel - below * pivot
                    right = right - below * pivot_right
                    for k in range(j + 1, PANEL):
                        columns[k] = columns[k] - below * (columns[k][j : j + 1, :] * inverse)
            done = jnp.where(col >= row + low, done, 0.0)
            upper[i, low:high, 0:rank] = done
            upper[i, low:high, rank:] = done_right
            if high < rank:
                a, b, c = split3(jnp.concatenate([done, done_right], 1))
                left = jnp.concatenate([a, b, c, a, b, a], 0)[:, 0:rank]
                both = jnp.concatenate([a, a, a, b, b, c], 0).astype(jnp.bfloat16)
                update = jnp.dot(
                    left.T.astype(jnp.bfloat16), both, preferred_element_type=jnp.float32
                )
                work[i, high:, :] = work[i, high:, :] - update[high:]

    full_row = lax.broadcasted_iota(jnp.int32, (rank, rank), 0)
    full_col = lax.broadcasted_iota(jnp.int32, (rank, rank), 1)
    for i in range(2):
        diagonal = jnp.where(full_row == full_col, upper[i, :, rank:], 0.0)
        coeffs_out[i : i + 1, :] = jnp.sum(diagonal, 0, keepdims=True)
    work[2, :, 0:rank] = upper[2, :, 0:rank].T
    rows = factor_out.shape[1]
    mine = pl.ds(pl.multiple_of(node * rows, rows), rows)
    factor_out[0] = work[2, mine, 0:rank]
    diagonal = jnp.where(
        full_row[0:rows] == full_col[0:rows], upper[2, mine, rank:], 0.0
    )
    top_coeffs_out[...] = jnp.sum(diagonal, 0, keepdims=True)[:, 0:rows]


def body(positions, charges, near_list, near_count, far_sample, proxies, strengths):
    blocks = lax.axis_size("leaf")
    nodes = lax.axis_size("node")
    size = charges.shape[0] // near_count.shape[0]
    rank = far_sample.shape[1]
    rows = rank // nodes
    vmem = pl.BlockSpec(memory_space=pltpu.VMEM)
    shape = lambda *dims: jax.ShapeDtypeStruct(dims, jnp.float32)
    window, gram, moment, top_gram, top_moment = pl.pallas_call(
        functools.partial(exchange_kernel, blocks, nodes),
        out_shape=(
            shape(9, 3, 4, size),
            shape(2, rank, rank),
            shape(2, 8, rank),
            shape(nodes, rows, rank),
            shape(1, rank),
        ),
        in_specs=[vmem] * 5,
        out_specs=(vmem,) * 5,
        scratch_shapes=[
            pltpu.VMEM((nodes, rows + 1, rank), jnp.float32),
            pltpu.VMEM((nodes, rows + 1, rank), jnp.float32),
            pltpu.SemaphoreType.DMA((18,)),
            pltpu.SemaphoreType.DMA((18,)),
            pltpu.SemaphoreType.DMA((nodes,)),
            pltpu.SemaphoreType.DMA((nodes,)),
            pltpu.SemaphoreType.DMA((nodes,)),
            pltpu.SemaphoreType.DMA((nodes,)),
        ],
        compiler_params=pltpu.CompilerParams(collective_id=0, has_side_effects=True),
        name="exchange",
    )(positions, charges[None, :], far_sample, proxies, strengths)
    smem = pl.BlockSpec(memory_space=pltpu.SMEM)
    near, coeffs, factor, top_coeffs = pl.pallas_call(
        leaf_kernel,
        out_shape=(shape(1, 2 * size), shape(2, rank), shape(1, rows, rank), shape(1, rows)),
        in_specs=[smem] + [vmem] * 6,
        out_specs=(vmem,) * 4,
        scratch_shapes=[
            pltpu.VMEM((2, size, 64), jnp.bfloat16),
            pltpu.VMEM((2, 32, 128), jnp.float32),
            pltpu.VMEM((2, size, 128), jnp.float32),
            pltpu.VMEM((3, rank, 2 * rank), jnp.float32),
            pltpu.VMEM((3, rank, 2 * rank), jnp.float32),
        ],
        name="leaf",
    )(near_count, near_list, window, gram, moment, top_gram, top_moment)
    return (near.reshape(-1), coeffs, factor, top_coeffs)


def solution(mesh):
    in_specs = (
        P(None, ("leaf", "node")),
        P(("leaf", "node")),
        P(("leaf", "node"), None),
        P(("leaf", "node")),
        P(("leaf", "node"), None),
        P(("leaf", "node"), None, None),
        P(("leaf", "node"), None),
    )
    out_specs = (
        P(("leaf", "node")),
        P(("leaf", "node"), None),
        P("leaf", "node", None),
        P("leaf", "node"),
    )
    return jax.shard_map(body, mesh=mesh, in_specs=in_specs, out_specs=out_specs, check_vma=False)
```

```python
import functools

import jax
import jax.numpy as jnp
from jax import lax
from jax.experimental import pallas as pl
from jax.experimental.pallas import tpu as pltpu
from jax.sharding import PartitionSpec as P

soft_square = 0.0025
ACROSS = 4
PANEL = 16
MESH = pl.DeviceIdType.MESH
HIGHEST = lax.Precision.HIGHEST


def split3(v):
    high = v.astype(jnp.bfloat16).astype(jnp.float32)
    rest = v - high
    mid = rest.astype(jnp.bfloat16).astype(jnp.float32)
    return high, mid, rest - mid


def feature_rows(xyz, fourth, fifth):
    row = lax.broadcasted_iota(jnp.int32, (8, xyz.shape[1]), 0)
    rows = jnp.where(row == 4, fifth, 0.0)
    rows = jnp.where(row == 3, fourth, rows)
    for k in range(3):
        rows = jnp.where(row == k, xyz[k : k + 1], rows)
    return split3(rows)


def source_features(xyz):
    high, mid, low = feature_rows(xyz, jnp.sum(xyz * xyz, 0, keepdims=True), 1.0)
    return jnp.concatenate([high, high, high, mid, mid, mid, low, low], 0).astype(jnp.bfloat16)


def target_features(xyz):
    norm = jnp.sum(xyz * xyz, 0, keepdims=True) + soft_square
    high, mid, low = feature_rows(-2.0 * xyz, 1.0, norm)
    return jnp.concatenate([high, mid, low, high, mid, low, high, mid], 0).T.astype(jnp.bfloat16)


def place(node):
    return node // 8, lax.rem(node // 2, ACROSS), lax.rem(node, 2)


def centre_of(block, node):
    slab, y, half = place(node)
    return (
        (2 * block + slab).astype(jnp.float32) + 0.5,
        y.astype(jnp.float32) + 0.5,
        (2 * half).astype(jnp.float32) + 1.0,
    )


def centred(rows, centre):
    row = lax.broadcasted_iota(jnp.int32, rows.shape, 0)
    shift = jnp.where(row == 0, centre[0], jnp.where(row == 1, centre[1], centre[2]))
    return rows - shift


def read_weights(block, node, near_ref, count_ref, weights):
    slab, y, half = place(node)
    row = lax.broadcasted_iota(jnp.int32, (32, near_ref.shape[1]), 0)
    lane = lax.broadcasted_iota(jnp.int32, (32, near_ref.shape[1]), 1)
    ids = jnp.full(row.shape, -1, jnp.int32)
    for k in range(27):
        ds, dy, w = k // 9 - 1, k // 3 % 3 - 1, k % 3
        z = 2 * half + w if w < 2 else 2 - half
        base = (2 * block + slab + ds) * ACROSS * ACROSS
        leaf = base + lax.rem(y + dy + ACROSS, ACROSS) * ACROSS + z
        ids = jnp.where(row == k, leaf, ids)
    for t in range(2):
        hit = (near_ref[t : t + 1, :] == ids) & (lane < count_ref[t])
        weight = jnp.sum(jnp.where(hit, 1.0, 0.0), 1, keepdims=True)
        own = row[:, 0:1] == 12 + t
        weights[t] = jnp.broadcast_to(jnp.where(own, 1.0, weight), (32, 128))


def add_tile(t, features, charges, weight, targets, totals):
    size = charges.shape[1]
    charges = charges * jnp.concatenate([weight] * (size // 128), 1)
    distance = jnp.dot(targets[t], features, preferred_element_type=jnp.float32)
    terms = lax.rsqrt(distance) * charges
    total = terms[:, 0:128]
    for k in range(1, size // 128):
        total = total + terms[:, k * 128 : (k + 1) * 128]
    totals[t] += total


def lane_sums(totals):
    ones = jnp.ones((8, totals.shape[1]), jnp.float32)
    return lax.dot_general(
        ones, totals, (((1,), (1,)), ((), ())), precision=HIGHEST, preferred_element_type=jnp.float32
    )[0:1]


def factorize(work, upper):
    count, rank = work.shape[0], work.shape[1]
    row = lax.broadcasted_iota(jnp.int32, (count, PANEL, rank), 1)
    col = lax.broadcasted_iota(jnp.int32, (count, PANEL, rank), 2)
    for low in range(0, rank, PANEL):
        high = low + PANEL
        panel = work[:, low:high, 0:rank]
        right = work[:, low:high, rank:]
        columns = [
            jnp.broadcast_to(panel[:, :, low + j : low + j + 1], (count, PANEL, rank))
            for j in range(PANEL)
        ]
        done = jnp.zeros((count, PANEL, rank), jnp.float32)
        done_right = done
        for j in range(PANEL):
            inverse = lax.rsqrt(columns[j][:, j : j + 1, :])
            below = jnp.where(row > j, columns[j] * inverse, 0.0)
            pivot = panel[:, j : j + 1] * inverse
            pivot_right = right[:, j : j + 1] * inverse
            done = jnp.where(row == j, pivot, done)
            done_right = jnp.where(row == j, pivot_right, done_right)
            if j + 1 < PANEL:
                panel = panel - below * pivot
                right = right - below * pivot_right
                for k in range(j + 1, PANEL):
                    columns[k] = columns[k] - below * (columns[k][:, j : j + 1, :] * inverse)
        done = jnp.where(col >= row + low, done, 0.0)
        upper[:, low:high, 0:rank] = done
        upper[:, low:high, rank:] = done_right
        if high < rank:
            for i in range(count):
                a, b, c = split3(jnp.concatenate([done[i], done_right[i]], 1))
                left = jnp.concatenate([a, b, c, a, b, a], 0)[:, 0:rank]
                both = jnp.concatenate([a, a, a, b, b, c], 0).astype(jnp.bfloat16)
                update = jnp.dot(
                    left.T.astype(jnp.bfloat16), both, preferred_element_type=jnp.float32
                )
                work[i, high:, :] = work[i, high:, :] - update[high:]


def diagonal_row(columns):
    row = lax.broadcasted_iota(jnp.int32, columns.shape, 0)
    col = lax.broadcasted_iota(jnp.int32, columns.shape, 1)
    return jnp.sum(jnp.where(row == col, columns, 0.0), 0, keepdims=True)


def exchange_kernel(
    blocks,
    nodes,
    count_ref,
    near_ref,
    pos_ref,
    charge_ref,
    far_ref,
    proxy_ref,
    strength_ref,
    near_out,
    coeffs_out,
    top_gram_ref,
    top_moment_ref,
    win_ref,
    targets,
    weights,
    totals,
    work,
    upper,
    share,
    parts,
    win_send,
    win_recv,
    rs_send,
    rs_recv,
    ag_send,
    ag_recv,
):
    block = lax.axis_index("leaf")
    node = lax.axis_index("node")
    slab, y, half = place(node)
    size = pos_ref.shape[1] // 2
    rank = far_ref.shape[1]

    def spatial(ds, dy, core):
        level = slab + ds
        step = (level + 2) // 2 - 1
        level = level - 2 * step
        other = level * 8 + lax.rem(y + dy + ACROSS, ACROSS) * 2 + core
        return (lax.rem(block + step + blocks, blocks), other)

    def in_block(k):
        return (block, lax.rem(node + k, nodes))

    outside = 1 - 2 * slab
    barrier = pltpu.get_barrier_semaphore()
    for k in range(1, nodes):
        pl.semaphore_signal(barrier, inc=1, device_id=in_block(k), device_id_type=MESH)
    for dy in (-1, 0, 1):
        for core in (0, 1):
            target = spatial(-outside, dy, core)
            pl.semaphore_signal(barrier, inc=1, device_id=target, device_id_type=MESH)

    for t in range(2):
        lanes = slice(t * size, (t + 1) * size)
        win_ref[4, t, 0:3, :] = pos_ref[:, lanes]
        win_ref[4, t, 3:4, :] = charge_ref[:, lanes]
    centre = centre_of(block, node)
    for t in range(2):
        lanes = slice(t * size, (t + 1) * size)
        targets[t] = target_features(centred(pos_ref[:, lanes], centre))
        distance = jnp.dot(
            targets[t],
            source_features(centred(proxy_ref[:, t, :], centre)),
            preferred_element_type=jnp.float32,
        )
        response = far_ref[lanes, :] + lax.rsqrt(distance) * strength_ref[t : t + 1, :]
        gram = lax.dot_general(
            response,
            response,
            (((0,), (0,)), ((), ())),
            precision=HIGHEST,
            preferred_element_type=jnp.float32,
        )
        moment = jnp.dot(
            jnp.broadcast_to(charge_ref[:, lanes], (8, size)),
            response,
            precision=HIGHEST,
            preferred_element_type=jnp.float32,
        )[0:1]
        work[t, :, 0:rank] = gram
        total = gram if t == 0 else total + gram
        total_moment = moment if t == 0 else total_moment + moment
        work[t, :, rank:] = jnp.broadcast_to(moment, (rank, rank)).T
    rows = rank // nodes
    for n in range(nodes):
        share[n, 0:rows, :] = total[n * rows : (n + 1) * rows]
        share[n, rows : rows + 1, :] = total_moment

    pl.semaphore_wait(barrier, nodes - 1 + 6)

    rs = []
    for k in range(1, nodes):
        target = in_block(k)
        rs.append(
            pltpu.make_async_remote_copy(
                src_ref=share.at[target[1]],
                dst_ref=parts.at[node],
                send_sem=rs_send.at[k],
                recv_sem=rs_recv.at[k],
                device_id=target,
                device_id_type=MESH,
            )
        )
        rs[-1].start()
    window = {}
    for ds in (-1, 0, 1):
        for dy in (-1, 0, 1):
            slot = 4 + 3 * ds + dy
            if slot != 4:
                window[slot, 0] = (
                    pltpu.make_async_remote_copy(
                        src_ref=win_ref.at[4, pl.ds(0, 2)],
                        dst_ref=win_ref.at[8 - slot, pl.ds(0, 2)],
                        send_sem=win_send.at[slot],
                        recv_sem=win_recv.at[slot],
                        device_id=spatial(ds, dy, half),
                        device_id_type=MESH,
                    )
                )
                window[slot, 0].start()
            window[slot, 1] = (
                pltpu.make_async_remote_copy(
                    src_ref=win_ref.at[4, pl.ds(1 - half, 1)],
                    dst_ref=win_ref.at[8 - slot, pl.ds(2, 1)],
                    send_sem=win_send.at[9 + slot],
                    recv_sem=win_recv.at[9 + slot],
                    device_id=spatial(ds, dy, 1 - half),
                    device_id_type=MESH,
                )
            )
            window[slot, 1].start()

    parts[node] = share[node]

    factorize(work, upper)
    for i in range(2):
        coeffs_out[i : i + 1, :] = diagonal_row(upper[i, :, rank:])
    read_weights(block, node, near_ref, count_ref, weights)
    totals[...] = jnp.zeros_like(totals)

    def add_source(slot, w):
        points = win_ref[slot, w]
        features = source_features(centred(points[0:3], centre))
        for t in (0, 1) if w < 2 else (1 - half,):
            k = slot * 3 + w
            add_tile(t, features, points[3:4], weights[t, k : k + 1, :], targets, totals)

    for w in range(2):
        add_source(4, w)

    for copy in rs:
        copy.wait_recv()
    sums = parts[0]
    for n in range(1, nodes):
        sums = sums + parts[n]
    top_gram_ref[node] = sums[0:rows]
    top_moment_ref[...] = sums[rows : rows + 1]
    ag = []
    for k in range(1, nodes):
        ag.append(
            pltpu.make_async_remote_copy(
                src_ref=top_gram_ref.at[node],
                dst_ref=top_gram_ref.at[node],
                send_sem=ag_send.at[k],
                recv_sem=ag_recv.at[k],
                device_id=in_block(k),
                device_id_type=MESH,
            )
        )
        ag[-1].start()

    for group in ((4, 3, 5), (0, 1, 2), (6, 7, 8)):
        for slot in group:
            for part in (0, 1):
                if (slot, part) in window:
                    window[8 - slot, part].wait_recv()
        for slot in group:
            for w in (2,) if slot == 4 else (0, 1, 2):
                add_source(slot, w)
    for t in range(2):
        near_out[:, t * size : (t + 1) * size] = lane_sums(totals[t])
    for copy in rs + list(window.values()):
        copy.wait_send()
    for copy in ag:
        copy.wait()


def top_kernel(
    near_ref,
    coeffs_ref,
    gram_ref,
    moment_ref,
    near_out,
    coeffs_out,
    factor_out,
    top_coeffs_out,
    work,
    upper,
):
    node = lax.axis_index("node")
    rank = work.shape[1]
    near_out[...] = near_ref[...]
    coeffs_out[...] = coeffs_ref[...]
    work[0, :, 0:rank] = gram_ref[...].reshape(rank, rank)
    work[0, :, rank:] = jnp.broadcast_to(moment_ref[...], (rank, rank)).T
    factorize(work, upper)
    work[0, :, 0:rank] = upper[0, :, 0:rank].T
    rows = factor_out.shape[1]
    mine = pl.ds(pl.multiple_of(node * rows, rows), rows)
    factor_out[0] = work[0, mine, 0:rank]
    top_coeffs_out[...] = diagonal_row(upper[0, mine, rank:])[:, 0:rows]


def body(positions, charges, near_list, near_count, far_sample, proxies, strengths):
    blocks = lax.axis_size("leaf")
    nodes = lax.axis_size("node")
    size = charges.shape[0] // near_count.shape[0]
    rank = far_sample.shape[1]
    rows = rank // nodes
    vmem = pl.BlockSpec(memory_space=pltpu.VMEM)
    smem = pl.BlockSpec(memory_space=pltpu.SMEM)
    shape = lambda *dims: jax.ShapeDtypeStruct(dims, jnp.float32)
    scratch = lambda *dims: pltpu.VMEM(dims, jnp.float32)
    semaphores = lambda n: pltpu.SemaphoreType.DMA((n,))
    near, coeffs, top_gram, top_moment = pl.pallas_call(
        functools.partial(exchange_kernel, blocks, nodes),
        out_shape=(
            shape(1, 2 * size),
            shape(2, rank),
            shape(nodes, rows, rank),
            shape(1, rank),
        ),
        in_specs=[smem] + [vmem] * 6,
        out_specs=(vmem,) * 4,
        scratch_shapes=[
            scratch(9, 3, 4, size),
            pltpu.VMEM((2, size, 64), jnp.bfloat16),
            scratch(2, 32, 128),
            scratch(2, size, 128),
            scratch(2, rank, 2 * rank),
            scratch(2, rank, 2 * rank),
            scratch(nodes, rows + 1, rank),
            scratch(nodes, rows + 1, rank),
            semaphores(18),
            semaphores(18),
            semaphores(nodes),
            semaphores(nodes),
            semaphores(nodes),
            semaphores(nodes),
        ],
        compiler_params=pltpu.CompilerParams(collective_id=0, has_side_effects=True),
        name="exchange",
    )(
        near_count,
        near_list,
        positions,
        charges[None, :],
        far_sample,
        jnp.transpose(proxies, (1, 0, 2)),
        strengths,
    )
    near, coeffs, factor, top_coeffs = pl.pallas_call(
        top_kernel,
        out_shape=(shape(1, 2 * size), shape(2, rank), shape(1, rows, rank), shape(1, rows)),
        in_specs=[vmem] * 4,
        out_specs=(vmem,) * 4,
        scratch_shapes=[scratch(1, rank, 2 * rank)] * 2,
        name="top",
    )(near, coeffs, top_gram, top_moment)
    return (near.reshape(-1), coeffs, factor, top_coeffs)


def solution(mesh):
    in_specs = (
        P(None, ("leaf", "node")),
        P(("leaf", "node")),
        P(("leaf", "node"), None),
        P(("leaf", "node")),
        P(("leaf", "node"), None),
        P(("leaf", "node"), None, None),
        P(("leaf", "node"), None),
    )
    out_specs = (
        P(("leaf", "node")),
        P(("leaf", "node"), None),
        P("leaf", "node", None),
        P("leaf", "node"),
    )
    return jax.shard_map(body, mesh=mesh, in_specs=in_specs, out_specs=out_specs, check_vma=False)
```

```python
import functools

import jax
import jax.numpy as jnp
from jax import lax
from jax.experimental import pallas as pl
from jax.experimental.pallas import tpu as pltpu
from jax.sharding import PartitionSpec as P

soft_square = 0.0025
ACROSS = 4
PANEL = 16
PIECE = 128
MESH = pl.DeviceIdType.MESH
HIGHEST = lax.Precision.HIGHEST
EARLY = 6
GROUPS = ((3, 5), (0, 1, 2), (6, 7, 8))


def split3(v):
    high = v.astype(jnp.bfloat16).astype(jnp.float32)
    rest = v - high
    mid = rest.astype(jnp.bfloat16).astype(jnp.float32)
    return high, mid, rest - mid


def feature_rows(xyz, fourth, fifth):
    row = lax.broadcasted_iota(jnp.int32, (8, xyz.shape[1]), 0)
    rows = jnp.where(row == 4, fifth, 0.0)
    rows = jnp.where(row == 3, fourth, rows)
    for k in range(3):
        rows = jnp.where(row == k, xyz[k : k + 1], rows)
    return split3(rows)


def source_features(xyz):
    high, mid, low = feature_rows(xyz, jnp.sum(xyz * xyz, 0, keepdims=True), 1.0)
    return jnp.concatenate([high, high, high, mid, mid, mid, low, low], 0).astype(jnp.bfloat16)


def target_features(xyz):
    norm = jnp.sum(xyz * xyz, 0, keepdims=True) + soft_square
    high, mid, low = feature_rows(-2.0 * xyz, 1.0, norm)
    return jnp.concatenate([high, mid, low, high, mid, low, high, mid], 0).T.astype(jnp.bfloat16)


def place(node):
    return node // 8, lax.rem(node // 2, ACROSS), lax.rem(node, 2)


def centre_of(block, node):
    slab, y, half = place(node)
    return (
        (2 * block + slab).astype(jnp.float32) + 0.5,
        y.astype(jnp.float32) + 0.5,
        (2 * half).astype(jnp.float32) + 1.0,
    )


def centred(rows, centre):
    row = lax.broadcasted_iota(jnp.int32, rows.shape, 0)
    shift = jnp.where(row == 0, centre[0], jnp.where(row == 1, centre[1], centre[2]))
    return rows - shift


def read_weights(block, node, near_ref, count_ref, weights):
    slab, y, half = place(node)
    row = lax.broadcasted_iota(jnp.int32, (32, near_ref.shape[1]), 0)
    lane = lax.broadcasted_iota(jnp.int32, (32, near_ref.shape[1]), 1)
    ids = jnp.full(row.shape, -1, jnp.int32)
    for k in range(27):
        ds, dy, w = k // 9 - 1, k // 3 % 3 - 1, k % 3
        z = 2 * half + w if w < 2 else 2 - half
        base = (2 * block + slab + ds) * ACROSS * ACROSS
        leaf = base + lax.rem(y + dy + ACROSS, ACROSS) * ACROSS + z
        ids = jnp.where(row == k, leaf, ids)
    for t in range(2):
        hit = (near_ref[t : t + 1, :] == ids) & (lane < count_ref[t])
        weight = jnp.sum(jnp.where(hit, 1.0, 0.0), 1, keepdims=True)
        own = row[:, 0:1] == 12 + t
        weights[t] = jnp.broadcast_to(jnp.where(own, 1.0, weight), (32, 128))


def near_work(sources, half, centre, win_ref, weights, targets, totals):
    size = win_ref.shape[3]

    def piece(t, rows, features, charges):
        distance = jnp.dot(targets[t, rows, :], features, preferred_element_type=jnp.float32)
        terms = lax.rsqrt(distance) * charges
        total = terms[:, 0:128]
        for k in range(1, size // 128):
            total = total + terms[:, k * 128 : (k + 1) * 128]
        totals[t, rows, :] += total

    for slot, w in sources:
        points = win_ref[slot, w]
        features = source_features(centred(points[0:3], centre))
        for t in (0, 1) if w < 2 else (1 - half,):
            weight = weights[t, slot * 3 + w : slot * 3 + w + 1, :]
            charges = points[3:4] * jnp.concatenate([weight] * (size // 128), 1)
            for start in range(0, size, PIECE):
                piece(t, slice(start, start + PIECE), features, charges)
                yield


def lane_sums(totals):
    ones = jnp.ones((8, totals.shape[1]), jnp.float32)
    return lax.dot_general(
        ones, totals, (((1,), (1,)), ((), ())), precision=HIGHEST, preferred_element_type=jnp.float32
    )[0:1]


def factorize(work, upper, panels, other=(), pieces=0):
    other = iter(other)
    pivots = len(panels) * PANEL
    steps = 0
    count, rank = work.shape[0], work.shape[1]
    row = lax.broadcasted_iota(jnp.int32, (count, PANEL, rank), 1)
    col = lax.broadcasted_iota(jnp.int32, (count, PANEL, rank), 2)
    for low in (p * PANEL for p in panels):
        high = low + PANEL
        panel = work[:, low:high, 0:rank]
        right = work[:, low:high, rank:]
        columns = [
            jnp.broadcast_to(panel[:, :, low + j : low + j + 1], (count, PANEL, rank))
            for j in range(PANEL)
        ]
        done = jnp.zeros((count, PANEL, rank), jnp.float32)
        done_right = done
        for j in range(PANEL):
            for _ in range(pieces * steps // pivots, pieces * (steps + 1) // pivots):
                next(other)
            steps += 1
            inverse = lax.rsqrt(columns[j][:, j : j + 1, :])
            below = jnp.where(row > j, columns[j] * inverse, 0.0)
            pivot = panel[:, j : j + 1] * inverse
            pivot_right = right[:, j : j + 1] * inverse
            done = jnp.where(row == j, pivot, done)
            done_right = jnp.where(row == j, pivot_right, done_right)
            if j + 1 < PANEL:
                panel = panel - below * pivot
                right = right - below * pivot_right
                for k in range(j + 1, PANEL):
                    columns[k] = columns[k] - below * (columns[k][:, j : j + 1, :] * inverse)
        done = jnp.where(col >= row + low, done, 0.0)
        upper[:, low:high, 0:rank] = done
        upper[:, low:high, rank:] = done_right
        if high < rank:
            for i in range(count):
                a, b, c = split3(jnp.concatenate([done[i], done_right[i]], 1))
                left = jnp.concatenate([a, b, c, a, b, a], 0)[:, 0:rank]
                both = jnp.concatenate([a, a, a, b, b, c], 0).astype(jnp.bfloat16)
                update = jnp.dot(
                    left.T.astype(jnp.bfloat16), both, preferred_element_type=jnp.float32
                )
                work[i, high:, :] = work[i, high:, :] - update[high:]


def diagonal_row(columns):
    row = lax.broadcasted_iota(jnp.int32, columns.shape, 0)
    col = lax.broadcasted_iota(jnp.int32, columns.shape, 1)
    return jnp.sum(jnp.where(row == col, columns, 0.0), 0, keepdims=True)


def exchange_kernel(
    blocks,
    nodes,
    count_ref,
    near_ref,
    pos_ref,
    charge_ref,
    far_hbm,
    proxy_ref,
    strength_ref,
    near_out,
    coeffs_out,
    top_gram_ref,
    top_moment_ref,
    win_ref,
    weights,
    far_ref,
    targets,
    totals,
    work,
    upper,
    share,
    parts,
    far_sem,
    win_send,
    win_recv,
    rs_send,
    rs_recv,
    ag_send,
    ag_recv,
):
    block = lax.axis_index("leaf")
    node = lax.axis_index("node")
    slab, y, half = place(node)
    size = pos_ref.shape[1] // 2
    rank = far_ref.shape[1]

    def spatial(ds, dy, core):
        level = slab + ds
        step = (level + 2) // 2 - 1
        level = level - 2 * step
        other = level * 8 + lax.rem(y + dy + ACROSS, ACROSS) * 2 + core
        return (lax.rem(block + step + blocks, blocks), other)

    def in_block(k):
        return (block, lax.rem(node + k, nodes))

    far_copies = []
    for t in range(2):
        lanes = pl.ds(t * size, size)
        far_copies.append(
            pltpu.make_async_copy(far_hbm.at[lanes], far_ref.at[lanes], far_sem.at[t])
        )
        far_copies[t].start()

    outside = 1 - 2 * slab
    barrier = pltpu.get_barrier_semaphore()
    for k in range(1, nodes):
        pl.semaphore_signal(barrier, inc=1, device_id=in_block(k), device_id_type=MESH)
    for dy in (-1, 0, 1):
        for core in (0, 1):
            target = spatial(-outside, dy, core)
            pl.semaphore_signal(barrier, inc=1, device_id=target, device_id_type=MESH)

    for t in range(2):
        lanes = slice(t * size, (t + 1) * size)
        win_ref[4, t, 0:3, :] = pos_ref[:, lanes]
        win_ref[4, t, 3:4, :] = charge_ref[:, lanes]
    centre = centre_of(block, node)
    for t in range(2):
        lanes = slice(t * size, (t + 1) * size)
        targets[t] = target_features(centred(pos_ref[:, lanes], centre))
        distance = jnp.dot(
            targets[t],
            source_features(centred(proxy_ref[:, t, :], centre)),
            preferred_element_type=jnp.float32,
        )
        far_copies[t].wait()
        response = far_ref[lanes, :] + lax.rsqrt(distance) * strength_ref[t : t + 1, :]
        gram = lax.dot_general(
            response,
            response,
            (((0,), (0,)), ((), ())),
            precision=HIGHEST,
            preferred_element_type=jnp.float32,
        )
        moment = jnp.dot(
            jnp.broadcast_to(charge_ref[:, lanes], (8, size)),
            response,
            precision=HIGHEST,
            preferred_element_type=jnp.float32,
        )[0:1]
        work[t, :, 0:rank] = gram
        total = gram if t == 0 else total + gram
        total_moment = moment if t == 0 else total_moment + moment
        work[t, :, rank:] = jnp.broadcast_to(moment, (rank, rank)).T
    rows = rank // nodes
    for n in range(nodes):
        share[n, 0:rows, :] = total[n * rows : (n + 1) * rows]
        share[n, rows : rows + 1, :] = total_moment

    pl.semaphore_wait(barrier, nodes - 1 + 6)

    rs = []
    for k in range(1, nodes):
        target = in_block(k)
        rs.append(
            pltpu.make_async_remote_copy(
                src_ref=share.at[target[1]],
                dst_ref=parts.at[node],
                send_sem=rs_send.at[k],
                recv_sem=rs_recv.at[k],
                device_id=target,
                device_id_type=MESH,
            )
        )
        rs[-1].start()
    window = {}
    for ds in (-1, 1, 0):
        for dy in (-1, 0, 1):
            slot = 4 + 3 * ds + dy
            if slot != 4:
                window[8 - slot] = pltpu.make_async_remote_copy(
                    src_ref=win_ref.at[4, pl.ds(0, 2)],
                    dst_ref=win_ref.at[8 - slot, pl.ds(0, 2)],
                    send_sem=win_send.at[8 - slot],
                    recv_sem=win_recv.at[8 - slot],
                    device_id=spatial(ds, dy, half),
                    device_id_type=MESH,
                )
                window[8 - slot].start()

    forwards = {}

    def forward(slot):
        forwards[slot] = pltpu.make_async_remote_copy(
            src_ref=win_ref.at[slot, pl.ds(1 - half, 1)],
            dst_ref=win_ref.at[slot, pl.ds(2, 1)],
            send_sem=win_send.at[9 + slot],
            recv_sem=win_recv.at[9 + slot],
            device_id=(block, node + 1 - 2 * half),
            device_id_type=MESH,
        )
        forwards[slot].start()

    forward(4)
    parts[node] = share[node]

    read_weights(block, node, near_ref, count_ref, weights)
    totals[...] = jnp.zeros_like(totals)

    def near(sources):
        return near_work(sources, half, centre, win_ref, weights, targets, totals)

    panels = range(rank // PANEL)
    factorize(work, upper, panels[:EARLY], near([(4, 0), (4, 1)]), 4 * (size // PIECE))

    for copy in rs:
        copy.wait_recv()
    sums = parts[0]
    for n in range(1, nodes):
        sums = sums + parts[n]
    top_gram_ref[node] = sums[0:rows]
    top_moment_ref[...] = sums[rows : rows + 1]
    ag = []
    for k in range(1, nodes):
        ag.append(
            pltpu.make_async_remote_copy(
                src_ref=top_gram_ref.at[node],
                dst_ref=top_gram_ref.at[node],
                send_sem=ag_send.at[k],
                recv_sem=ag_recv.at[k],
                device_id=in_block(k),
                device_id_type=MESH,
            )
        )
        ag[-1].start()

    late = (4,)
    for group in GROUPS:
        for slot in group:
            window[slot].wait_recv()
            forward(slot)
        for slot in late:
            forwards[slot].wait_recv()
        sources = [(slot, 2) for slot in late]
        if group != GROUPS[-1]:
            sources += [(slot, w) for slot in group for w in range(2)]
        work_left = near(sources)
        if group == GROUPS[0]:
            tiles = len(late) + 4 * len(group)
            factorize(work, upper, panels[EARLY:], work_left, tiles * (size // PIECE))
            for i in range(2):
                coeffs_out[i : i + 1, :] = diagonal_row(upper[i, :, rank:])
        for _ in work_left:
            pass
        late = group
    for t in range(2):
        near_out[:, t * size : (t + 1) * size] = lane_sums(totals[t])
    for slot in late:
        forwards[slot].wait_recv()
    for copy in rs + list(window.values()) + list(forwards.values()):
        copy.wait_send()
    for copy in ag:
        copy.wait()


def top_kernel(
    near_ref,
    coeffs_ref,
    gram_ref,
    moment_ref,
    win_ref,
    weights,
    near_out,
    coeffs_out,
    factor_out,
    top_coeffs_out,
    targets,
    totals,
    work,
    upper,
):
    block = lax.axis_index("leaf")
    node = lax.axis_index("node")
    half = place(node)[2]
    centre = centre_of(block, node)
    rank = work.shape[1]
    size = win_ref.shape[3]
    for t in range(2):
        targets[t] = target_features(centred(win_ref[4, t, 0:3, :], centre))
    totals[...] = jnp.zeros_like(totals)
    sources = [(slot, w) for slot in GROUPS[-1] for w in range(3)]
    near = near_work(sources, half, centre, win_ref, weights, targets, totals)
    pieces = 5 * len(GROUPS[-1]) * (size // PIECE)

    coeffs_out[...] = coeffs_ref[...]
    work[0, :, 0:rank] = gram_ref[...].reshape(rank, rank)
    work[0, :, rank:] = jnp.broadcast_to(moment_ref[...], (rank, rank)).T
    factorize(work, upper, range(rank // PANEL), near, pieces)
    for t in range(2):
        lanes = slice(t * size, (t + 1) * size)
        near_out[:, lanes] = near_ref[:, lanes] + lane_sums(totals[t])
    work[0, :, 0:rank] = upper[0, :, 0:rank].T
    rows = factor_out.shape[1]
    mine = pl.ds(pl.multiple_of(node * rows, rows), rows)
    factor_out[0] = work[0, mine, 0:rank]
    top_coeffs_out[...] = diagonal_row(upper[0, mine, rank:])[:, 0:rows]


def body(positions, charges, near_list, near_count, far_sample, proxies, strengths):
    blocks = lax.axis_size("leaf")
    nodes = lax.axis_size("node")
    size = charges.shape[0] // near_count.shape[0]
    rank = far_sample.shape[1]
    rows = rank // nodes
    vmem = pl.BlockSpec(memory_space=pltpu.VMEM)
    smem = pl.BlockSpec(memory_space=pltpu.SMEM)
    shape = lambda *dims: jax.ShapeDtypeStruct(dims, jnp.float32)
    scratch = lambda *dims: pltpu.VMEM(dims, jnp.float32)
    semaphores = lambda n: pltpu.SemaphoreType.DMA((n,))
    near, coeffs, top_gram, top_moment, window, weights = pl.pallas_call(
        functools.partial(exchange_kernel, blocks, nodes),
        out_shape=(
            shape(1, 2 * size),
            shape(2, rank),
            shape(nodes, rows, rank),
            shape(1, rank),
            shape(9, 3, 4, size),
            shape(2, 32, 128),
        ),
        in_specs=[smem] + [vmem] * 3 + [pl.BlockSpec(memory_space=pl.ANY)] + [vmem] * 2,
        out_specs=(vmem,) * 6,
        scratch_shapes=[
            scratch(2 * size, rank),
            pltpu.VMEM((2, size, 64), jnp.bfloat16),
            scratch(2, size, 128),
            scratch(2, rank, 2 * rank),
            scratch(2, rank, 2 * rank),
            scratch(nodes, rows + 1, rank),
            scratch(nodes, rows + 1, rank),
            semaphores(2),
            semaphores(18),
            semaphores(18),
            semaphores(nodes),
            semaphores(nodes),
            semaphores(nodes),
            semaphores(nodes),
        ],
        compiler_params=pltpu.CompilerParams(collective_id=0, has_side_effects=True),
        name="exchange",
    )(
        near_count,
        near_list,
        positions,
        charges[None, :],
        far_sample,
        jnp.transpose(proxies, (1, 0, 2)),
        strengths,
    )
    near, coeffs, factor, top_coeffs = pl.pallas_call(
        top_kernel,
        out_shape=(shape(1, 2 * size), shape(2, rank), shape(1, rows, rank), shape(1, rows)),
        in_specs=[vmem] * 6,
        out_specs=(vmem,) * 4,
        scratch_shapes=[
            pltpu.VMEM((2, size, 64), jnp.bfloat16),
            scratch(2, size, 128),
            scratch(1, rank, 2 * rank),
            scratch(1, rank, 2 * rank),
        ],
        name="top",
    )(near, coeffs, top_gram, top_moment, window, weights)
    return (near.reshape(-1), coeffs, factor, top_coeffs)


def solution(mesh):
    in_specs = (
        P(None, ("leaf", "node")),
        P(("leaf", "node")),
        P(("leaf", "node"), None),
        P(("leaf", "node")),
        P(("leaf", "node"), None),
        P(("leaf", "node"), None, None),
        P(("leaf", "node"), None),
    )
    out_specs = (
        P(("leaf", "node")),
        P(("leaf", "node"), None),
        P("leaf", "node", None),
        P("leaf", "node"),
    )
    return jax.shard_map(body, mesh=mesh, in_specs=in_specs, out_specs=out_specs, check_vma=False)
```

```python
import functools

import jax
import jax.numpy as jnp
from jax import lax
from jax.experimental import pallas as pl
from jax.experimental.pallas import tpu as pltpu
from jax.sharding import PartitionSpec as P

soft_square = 0.0025
ACROSS = 4
PANEL = 16
PIECE = 128
MESH = pl.DeviceIdType.MESH
HIGHEST = lax.Precision.HIGHEST
EARLY = 6
GROUPS = ((3, 5), (0, 1, 2), (6, 7, 8))


def split3(v):
    high = v.astype(jnp.bfloat16).astype(jnp.float32)
    rest = v - high
    mid = rest.astype(jnp.bfloat16).astype(jnp.float32)
    return high, mid, rest - mid


def feature_rows(xyz, fourth, fifth):
    row = lax.broadcasted_iota(jnp.int32, (8, xyz.shape[1]), 0)
    rows = jnp.where(row == 4, fifth, 0.0)
    rows = jnp.where(row == 3, fourth, rows)
    for k in range(3):
        rows = jnp.where(row == k, xyz[k : k + 1], rows)
    return split3(rows)


def source_features(xyz):
    high, mid, low = feature_rows(xyz, jnp.sum(xyz * xyz, 0, keepdims=True), 1.0)
    return jnp.concatenate([high, high, high, mid, mid, mid, low, low], 0).astype(jnp.bfloat16)


def target_features(xyz):
    norm = jnp.sum(xyz * xyz, 0, keepdims=True) + soft_square
    high, mid, low = feature_rows(-2.0 * xyz, 1.0, norm)
    return jnp.concatenate([high, mid, low, high, mid, low, high, mid], 0).T.astype(jnp.bfloat16)


def place(node):
    return node // 8, lax.rem(node // 2, ACROSS), lax.rem(node, 2)


def centre_of(block, node):
    slab, y, half = place(node)
    return (
        (2 * block + slab).astype(jnp.float32) + 0.5,
        y.astype(jnp.float32) + 0.5,
        (2 * half).astype(jnp.float32) + 1.0,
    )


def centred(rows, centre):
    row = lax.broadcasted_iota(jnp.int32, rows.shape, 0)
    shift = jnp.where(row == 0, centre[0], jnp.where(row == 1, centre[1], centre[2]))
    return rows - shift


def read_weights(block, node, near_ref, count_ref, weights):
    slab, y, half = place(node)
    row = lax.broadcasted_iota(jnp.int32, (32, near_ref.shape[1]), 0)
    lane = lax.broadcasted_iota(jnp.int32, (32, near_ref.shape[1]), 1)
    ids = jnp.full(row.shape, -1, jnp.int32)
    for k in range(27):
        ds, dy, w = k // 9 - 1, k // 3 % 3 - 1, k % 3
        z = 2 * half + w if w < 2 else 2 - half
        base = (2 * block + slab + ds) * ACROSS * ACROSS
        leaf = base + lax.rem(y + dy + ACROSS, ACROSS) * ACROSS + z
        ids = jnp.where(row == k, leaf, ids)
    for t in range(2):
        hit = (near_ref[t : t + 1, :] == ids) & (lane < count_ref[t])
        weight = jnp.sum(jnp.where(hit, 1.0, 0.0), 1, keepdims=True)
        own = row[:, 0:1] == 12 + t
        weights[t] = jnp.broadcast_to(jnp.where(own, 1.0, weight), (32, 128))


def near_work(sources, half, centre, win_ref, weights, targets, totals):
    size = win_ref.shape[3]

    def piece(t, rows, features, charges):
        distance = jnp.dot(targets[t, rows, :], features, preferred_element_type=jnp.float32)
        terms = lax.rsqrt(distance) * charges
        total = terms[:, 0:128]
        for k in range(1, size // 128):
            total = total + terms[:, k * 128 : (k + 1) * 128]
        totals[t, rows, :] += total

    for slot, w in sources:
        points = win_ref[slot, w]
        features = source_features(centred(points[0:3], centre))
        for t in (0, 1) if w < 2 else (1 - half,):
            weight = weights[t, slot * 3 + w : slot * 3 + w + 1, :]
            charges = points[3:4] * jnp.concatenate([weight] * (size // 128), 1)
            for start in range(0, size, PIECE):
                piece(t, slice(start, start + PIECE), features, charges)
                yield


def lane_sums(totals):
    ones = jnp.ones((8, totals.shape[1]), jnp.float32)
    return lax.dot_general(
        ones, totals, (((1,), (1,)), ((), ())), precision=HIGHEST, preferred_element_type=jnp.float32
    )[0:1]


def factorize(work, upper, panels, other=(), pieces=0):
    other = iter(other)
    pivots = len(panels) * PANEL
    steps = 0
    count, rank = work.shape[0], work.shape[1]
    row = lax.broadcasted_iota(jnp.int32, (count, PANEL, rank), 1)
    col = lax.broadcasted_iota(jnp.int32, (count, PANEL, rank), 2)

    def spread(rows, low):
        return [
            jnp.broadcast_to(rows[:, :, low + j : low + j + 1], (count, PANEL, rank))
            for j in range(PANEL)
        ]

    low = panels[0] * PANEL
    panel = work[:, low : low + PANEL, 0:rank]
    right = work[:, low : low + PANEL, rank:]
    for low in (p * PANEL for p in panels):
        high = low + PANEL
        columns = spread(panel, low)
        if high < rank:
            after = work[:, high : high + PANEL, 0:rank]
            after_right = work[:, high : high + PANEL, rank:]
            after_columns = spread(after, low)
        done = jnp.zeros((count, PANEL, rank), jnp.float32)
        done_right = done
        for j in range(PANEL):
            for _ in range(pieces * steps // pivots, pieces * (steps + 1) // pivots):
                next(other)
            steps += 1
            inverse = lax.rsqrt(columns[j][:, j : j + 1, :])
            below = jnp.where(row > j, columns[j] * inverse, 0.0)
            pivot = panel[:, j : j + 1] * inverse
            pivot_right = right[:, j : j + 1] * inverse
            done = jnp.where(row == j, pivot, done)
            done_right = jnp.where(row == j, pivot_right, done_right)
            scaled = [columns[k][:, j : j + 1, :] * inverse for k in range(j + 1, PANEL)]
            if j + 1 < PANEL:
                panel = panel - below * pivot
                right = right - below * pivot_right
                for k in range(j + 1, PANEL):
                    columns[k] = columns[k] - below * scaled[k - j - 1]
            if high < rank:
                further = after_columns[j] * inverse
                after = after - further * pivot
                after_right = after_right - further * pivot_right
                for k in range(j + 1, PANEL):
                    after_columns[k] = after_columns[k] - further * scaled[k - j - 1]
        done = jnp.where(col >= row + low, done, 0.0)
        upper[:, low:high, 0:rank] = done
        upper[:, low:high, rank:] = done_right
        if high < rank:
            panel, right = after, after_right
        rest = high + PANEL
        if rest < rank:
            for i in range(count):
                a, b, c = split3(jnp.concatenate([done[i], done_right[i]], 1))
                left = jnp.concatenate([a, b, c, a, b, a], 0)[:, 0:rank]
                both = jnp.concatenate([a, a, a, b, b, c], 0).astype(jnp.bfloat16)
                update = jnp.dot(
                    left.T.astype(jnp.bfloat16), both, preferred_element_type=jnp.float32
                )
                work[i, rest:, :] = work[i, rest:, :] - update[rest:]
    if high < rank:
        work[:, high : high + PANEL, 0:rank] = panel
        work[:, high : high + PANEL, rank:] = right


def diagonal_row(columns):
    row = lax.broadcasted_iota(jnp.int32, columns.shape, 0)
    col = lax.broadcasted_iota(jnp.int32, columns.shape, 1)
    return jnp.sum(jnp.where(row == col, columns, 0.0), 0, keepdims=True)


def exchange_kernel(
    blocks,
    nodes,
    count_ref,
    near_ref,
    pos_ref,
    charge_ref,
    far_hbm,
    proxy_ref,
    strength_ref,
    near_out,
    coeffs_out,
    top_gram_ref,
    top_moment_ref,
    win_ref,
    weights,
    far_ref,
    targets,
    totals,
    work,
    upper,
    share,
    parts,
    far_sem,
    win_send,
    win_recv,
    rs_send,
    rs_recv,
    ag_send,
    ag_recv,
):
    block = lax.axis_index("leaf")
    node = lax.axis_index("node")
    slab, y, half = place(node)
    size = pos_ref.shape[1] // 2
    rank = far_ref.shape[1]

    def spatial(ds, dy, core):
        level = slab + ds
        step = (level + 2) // 2 - 1
        level = level - 2 * step
        other = level * 8 + lax.rem(y + dy + ACROSS, ACROSS) * 2 + core
        return (lax.rem(block + step + blocks, blocks), other)

    def in_block(k):
        return (block, lax.rem(node + k, nodes))

    far_copies = []
    for t in range(2):
        lanes = pl.ds(t * size, size)
        far_copies.append(
            pltpu.make_async_copy(far_hbm.at[lanes], far_ref.at[lanes], far_sem.at[t])
        )
        far_copies[t].start()

    outside = 1 - 2 * slab
    barrier = pltpu.get_barrier_semaphore()
    for k in range(1, nodes):
        pl.semaphore_signal(barrier, inc=1, device_id=in_block(k), device_id_type=MESH)
    for dy in (-1, 0, 1):
        for core in (0, 1):
            target = spatial(-outside, dy, core)
            pl.semaphore_signal(barrier, inc=1, device_id=target, device_id_type=MESH)

    for t in range(2):
        lanes = slice(t * size, (t + 1) * size)
        win_ref[4, t, 0:3, :] = pos_ref[:, lanes]
        win_ref[4, t, 3:4, :] = charge_ref[:, lanes]
    centre = centre_of(block, node)
    for t in range(2):
        lanes = slice(t * size, (t + 1) * size)
        targets[t] = target_features(centred(pos_ref[:, lanes], centre))
        distance = jnp.dot(
            targets[t],
            source_features(centred(proxy_ref[:, t, :], centre)),
            preferred_element_type=jnp.float32,
        )
        far_copies[t].wait()
        response = far_ref[lanes, :] + lax.rsqrt(distance) * strength_ref[t : t + 1, :]
        gram = lax.dot_general(
            response,
            response,
            (((0,), (0,)), ((), ())),
            precision=HIGHEST,
            preferred_element_type=jnp.float32,
        )
        moment = jnp.dot(
            jnp.broadcast_to(charge_ref[:, lanes], (8, size)),
            response,
            precision=HIGHEST,
            preferred_element_type=jnp.float32,
        )[0:1]
        work[t, :, 0:rank] = gram
        total = gram if t == 0 else total + gram
        total_moment = moment if t == 0 else total_moment + moment
        work[t, :, rank:] = jnp.broadcast_to(moment, (rank, rank)).T
    rows = rank // nodes
    for n in range(nodes):
        share[n, 0:rows, :] = total[n * rows : (n + 1) * rows]
        share[n, rows : rows + 1, :] = total_moment

    pl.semaphore_wait(barrier, nodes - 1 + 6)

    rs = []
    for k in range(1, nodes):
        target = in_block(k)
        rs.append(
            pltpu.make_async_remote_copy(
                src_ref=share.at[target[1]],
                dst_ref=parts.at[node],
                send_sem=rs_send.at[k],
                recv_sem=rs_recv.at[k],
                device_id=target,
                device_id_type=MESH,
            )
        )
        rs[-1].start()
    window = {}
    for ds in (-1, 1, 0):
        for dy in (-1, 0, 1):
            slot = 4 + 3 * ds + dy
            if slot != 4:
                window[8 - slot] = pltpu.make_async_remote_copy(
                    src_ref=win_ref.at[4, pl.ds(0, 2)],
                    dst_ref=win_ref.at[8 - slot, pl.ds(0, 2)],
                    send_sem=win_send.at[8 - slot],
                    recv_sem=win_recv.at[8 - slot],
                    device_id=spatial(ds, dy, half),
                    device_id_type=MESH,
                )
                window[8 - slot].start()

    forwards = {}

    def forward(slot):
        forwards[slot] = pltpu.make_async_remote_copy(
            src_ref=win_ref.at[slot, pl.ds(1 - half, 1)],
            dst_ref=win_ref.at[slot, pl.ds(2, 1)],
            send_sem=win_send.at[9 + slot],
            recv_sem=win_recv.at[9 + slot],
            device_id=(block, node + 1 - 2 * half),
            device_id_type=MESH,
        )
        forwards[slot].start()

    forward(4)
    parts[node] = share[node]

    read_weights(block, node, near_ref, count_ref, weights)
    totals[...] = jnp.zeros_like(totals)

    def near(sources):
        return near_work(sources, half, centre, win_ref, weights, targets, totals)

    panels = range(rank // PANEL)
    factorize(work, upper, panels[:EARLY], near([(4, 0), (4, 1)]), 4 * (size // PIECE))

    for copy in rs:
        copy.wait_recv()
    sums = parts[0]
    for n in range(1, nodes):
        sums = sums + parts[n]
    top_gram_ref[node] = sums[0:rows]
    top_moment_ref[...] = sums[rows : rows + 1]
    ag = []
    for k in range(1, nodes):
        ag.append(
            pltpu.make_async_remote_copy(
                src_ref=top_gram_ref.at[node],
                dst_ref=top_gram_ref.at[node],
                send_sem=ag_send.at[k],
                recv_sem=ag_recv.at[k],
                device_id=in_block(k),
                device_id_type=MESH,
            )
        )
        ag[-1].start()

    late = (4,)
    for group in GROUPS:
        for slot in group:
            window[slot].wait_recv()
            forward(slot)
        for slot in late:
            forwards[slot].wait_recv()
        sources = [(slot, 2) for slot in late]
        sources += [(slot, w) for slot in group for w in range(2)]
        work_left = near(sources)
        if group == GROUPS[0]:
            tiles = len(late) + 4 * len(group)
            factorize(work, upper, panels[EARLY:], work_left, tiles * (size // PIECE))
            for i in range(2):
                coeffs_out[i : i + 1, :] = diagonal_row(upper[i, :, rank:])
        for _ in work_left:
            pass
        late = group
    for slot in late:
        forwards[slot].wait_recv()
    for _ in near([(slot, 2) for slot in late]):
        pass
    for t in range(2):
        near_out[:, t * size : (t + 1) * size] = lane_sums(totals[t])
    for copy in rs + list(window.values()) + list(forwards.values()):
        copy.wait_send()
    for copy in ag:
        copy.wait()


def top_kernel(
    near_ref,
    coeffs_ref,
    gram_ref,
    moment_ref,
    near_out,
    coeffs_out,
    factor_out,
    top_coeffs_out,
    work,
    upper,
):
    node = lax.axis_index("node")
    rank = work.shape[1]
    near_out[...] = near_ref[...]
    coeffs_out[...] = coeffs_ref[...]
    work[0, :, 0:rank] = gram_ref[...].reshape(rank, rank)
    work[0, :, rank:] = jnp.broadcast_to(moment_ref[...], (rank, rank)).T
    factorize(work, upper, range(rank // PANEL))
    work[0, :, 0:rank] = upper[0, :, 0:rank].T
    rows = factor_out.shape[1]
    mine = pl.ds(pl.multiple_of(node * rows, rows), rows)
    factor_out[0] = work[0, mine, 0:rank]
    top_coeffs_out[...] = diagonal_row(upper[0, mine, rank:])[:, 0:rows]


def body(positions, charges, near_list, near_count, far_sample, proxies, strengths):
    blocks = lax.axis_size("leaf")
    nodes = lax.axis_size("node")
    size = charges.shape[0] // near_count.shape[0]
    rank = far_sample.shape[1]
    rows = rank // nodes
    vmem = pl.BlockSpec(memory_space=pltpu.VMEM)
    smem = pl.BlockSpec(memory_space=pltpu.SMEM)
    shape = lambda *dims: jax.ShapeDtypeStruct(dims, jnp.float32)
    scratch = lambda *dims: pltpu.VMEM(dims, jnp.float32)
    semaphores = lambda n: pltpu.SemaphoreType.DMA((n,))
    near, coeffs, top_gram, top_moment = pl.pallas_call(
        functools.partial(exchange_kernel, blocks, nodes),
        out_shape=(
            shape(1, 2 * size),
            shape(2, rank),
            shape(nodes, rows, rank),
            shape(1, rank),
        ),
        in_specs=[smem] + [vmem] * 3 + [pl.BlockSpec(memory_space=pl.ANY)] + [vmem] * 2,
        out_specs=(vmem,) * 4,
        scratch_shapes=[
            scratch(9, 3, 4, size),
            scratch(2, 32, 128),
            scratch(2 * size, rank),
            pltpu.VMEM((2, size, 64), jnp.bfloat16),
            scratch(2, size, 128),
            scratch(2, rank, 2 * rank),
            scratch(2, rank, 2 * rank),
            scratch(nodes, rows + 1, rank),
            scratch(nodes, rows + 1, rank),
            semaphores(2),
            semaphores(18),
            semaphores(18),
            semaphores(nodes),
            semaphores(nodes),
            semaphores(nodes),
            semaphores(nodes),
        ],
        compiler_params=pltpu.CompilerParams(collective_id=0, has_side_effects=True),
        name="exchange",
    )(
        near_count,
        near_list,
        positions,
        charges[None, :],
        far_sample,
        jnp.transpose(proxies, (1, 0, 2)),
        strengths,
    )
    near, coeffs, factor, top_coeffs = pl.pallas_call(
        top_kernel,
        out_shape=(shape(1, 2 * size), shape(2, rank), shape(1, rows, rank), shape(1, rows)),
        in_specs=[vmem] * 4,
        out_specs=(vmem,) * 4,
        scratch_shapes=[
            scratch(1, rank, 2 * rank),
            scratch(1, rank, 2 * rank),
        ],
        name="top",
    )(near, coeffs, top_gram, top_moment)
    return (near.reshape(-1), coeffs, factor, top_coeffs)


def solution(mesh):
    in_specs = (
        P(None, ("leaf", "node")),
        P(("leaf", "node")),
        P(("leaf", "node"), None),
        P(("leaf", "node")),
        P(("leaf", "node"), None),
        P(("leaf", "node"), None, None),
        P(("leaf", "node"), None),
    )
    out_specs = (
        P(("leaf", "node")),
        P(("leaf", "node"), None),
        P("leaf", "node", None),
        P("leaf", "node"),
    )
    return jax.shard_map(body, mesh=mesh, in_specs=in_specs, out_specs=out_specs, check_vma=False)
```

```python
import functools

import jax
import jax.numpy as jnp
from jax import lax
from jax.experimental import pallas as pl
from jax.experimental.pallas import tpu as pltpu
from jax.sharding import PartitionSpec as P

soft_square = 0.0025
ACROSS = 4
PANEL = 16
PIECE = 128
MESH = pl.DeviceIdType.MESH
HIGHEST = lax.Precision.HIGHEST
LATE = ((8, 0), (8, 1), (8, 2))
EARLY = 7
GROUPS = ((3, 5), (0, 1, 2), (6, 7, 8))


def split3(v):
    high = v.astype(jnp.bfloat16).astype(jnp.float32)
    rest = v - high
    mid = rest.astype(jnp.bfloat16).astype(jnp.float32)
    return high, mid, rest - mid


def feature_rows(xyz, fourth, fifth):
    row = lax.broadcasted_iota(jnp.int32, (8, xyz.shape[1]), 0)
    rows = jnp.where(row == 4, fifth, 0.0)
    rows = jnp.where(row == 3, fourth, rows)
    for k in range(3):
        rows = jnp.where(row == k, xyz[k : k + 1], rows)
    return split3(rows)


def source_features(xyz):
    high, mid, low = feature_rows(xyz, jnp.sum(xyz * xyz, 0, keepdims=True), 1.0)
    return jnp.concatenate([high, high, high, mid, mid, mid, low, low], 0).astype(jnp.bfloat16)


def target_features(xyz):
    norm = jnp.sum(xyz * xyz, 0, keepdims=True) + soft_square
    high, mid, low = feature_rows(-2.0 * xyz, 1.0, norm)
    return jnp.concatenate([high, mid, low, high, mid, low, high, mid], 0).T.astype(jnp.bfloat16)


def place(node):
    return node // 8, lax.rem(node // 2, ACROSS), lax.rem(node, 2)


def centre_of(block, node):
    slab, y, half = place(node)
    return (
        (2 * block + slab).astype(jnp.float32) + 0.5,
        y.astype(jnp.float32) + 0.5,
        (2 * half).astype(jnp.float32) + 1.0,
    )


def centred(rows, centre):
    row = lax.broadcasted_iota(jnp.int32, rows.shape, 0)
    shift = jnp.where(row == 0, centre[0], jnp.where(row == 1, centre[1], centre[2]))
    return rows - shift


def read_weights(block, node, near_ref, count_ref, weights):
    slab, y, half = place(node)
    row = lax.broadcasted_iota(jnp.int32, (32, near_ref.shape[1]), 0)
    lane = lax.broadcasted_iota(jnp.int32, (32, near_ref.shape[1]), 1)
    ids = jnp.full(row.shape, -1, jnp.int32)
    for k in range(27):
        ds, dy, w = k // 9 - 1, k // 3 % 3 - 1, k % 3
        z = 2 * half + w if w < 2 else 2 - half
        base = (2 * block + slab + ds) * ACROSS * ACROSS
        leaf = base + lax.rem(y + dy + ACROSS, ACROSS) * ACROSS + z
        ids = jnp.where(row == k, leaf, ids)
    for t in range(2):
        hit = (near_ref[t : t + 1, :] == ids) & (lane < count_ref[0:1, t : t + 1])
        weight = jnp.sum(jnp.where(hit, 1.0, 0.0), 1, keepdims=True)
        own = row[:, 0:1] == 12 + t
        weights[t] = jnp.broadcast_to(jnp.where(own, 1.0, weight), (32, 128))


def near_work(sources, half, centre, win_ref, weights, targets, totals):
    size = win_ref.shape[3]

    def piece(t, rows, features, charges):
        distance = jnp.dot(targets[t, rows, :], features, preferred_element_type=jnp.float32)
        terms = lax.rsqrt(distance) * charges
        total = terms[:, 0:128]
        for k in range(1, size // 128):
            total = total + terms[:, k * 128 : (k + 1) * 128]
        totals[t, rows, :] += total

    for slot, w in sources:
        points = win_ref[slot, w]
        features = source_features(centred(points[0:3], centre))
        for t in (0, 1) if w < 2 else (1 - half,):
            weight = weights[t, slot * 3 + w : slot * 3 + w + 1, :]
            charges = points[3:4] * jnp.concatenate([weight] * (size // 128), 1)
            for start in range(0, size, PIECE):
                piece(t, slice(start, start + PIECE), features, charges)
                yield


def lane_sums(totals):
    ones = jnp.ones((8, totals.shape[1]), jnp.float32)
    return lax.dot_general(
        ones, totals, (((1,), (1,)), ((), ())), precision=HIGHEST, preferred_element_type=jnp.float32
    )[0:1]


def factorize(work, upper, panels, other=(), pieces=0):
    other = iter(other)
    pivots = len(panels) * PANEL
    steps = 0
    count, rank = work.shape[0], work.shape[1]
    row = lax.broadcasted_iota(jnp.int32, (count, PANEL, rank), 1)
    col = lax.broadcasted_iota(jnp.int32, (count, PANEL, rank), 2)

    def spread(rows, low):
        return [
            jnp.broadcast_to(rows[:, :, low + j : low + j + 1], (count, PANEL, rank))
            for j in range(PANEL)
        ]

    low = panels[0] * PANEL
    panel = work[:, low : low + PANEL, 0:rank]
    right = work[:, low : low + PANEL, rank:]
    for low in (p * PANEL for p in panels):
        high = low + PANEL
        columns = spread(panel, low)
        if high < rank:
            after = work[:, high : high + PANEL, 0:rank]
            after_right = work[:, high : high + PANEL, rank:]
            after_columns = spread(after, low)
        done = jnp.zeros((count, PANEL, rank), jnp.float32)
        done_right = done
        for j in range(PANEL):
            for _ in range(pieces * steps // pivots, pieces * (steps + 1) // pivots):
                next(other)
            steps += 1
            inverse = lax.rsqrt(columns[j][:, j : j + 1, :])
            below = jnp.where(row > j, columns[j] * inverse, 0.0)
            pivot = panel[:, j : j + 1] * inverse
            pivot_right = right[:, j : j + 1] * inverse
            done = jnp.where(row == j, pivot, done)
            done_right = jnp.where(row == j, pivot_right, done_right)
            scaled = [columns[k][:, j : j + 1, :] * inverse for k in range(j + 1, PANEL)]
            if j + 1 < PANEL:
                panel = panel - below * pivot
                right = right - below * pivot_right
                for k in range(j + 1, PANEL):
                    columns[k] = columns[k] - below * scaled[k - j - 1]
            if high < rank:
                further = after_columns[j] * inverse
                after = after - further * pivot
                after_right = after_right - further * pivot_right
                for k in range(j + 1, PANEL):
                    after_columns[k] = after_columns[k] - further * scaled[k - j - 1]
        done = jnp.where(col >= row + low, done, 0.0)
        upper[:, low:high, 0:rank] = done
        upper[:, low:high, rank:] = done_right
        if high < rank:
            panel, right = after, after_right
        rest = high + PANEL
        if rest < rank:
            for i in range(count):
                a, b, c = split3(jnp.concatenate([done[i], done_right[i]], 1))
                left = jnp.concatenate([a, b, c, a, b, a], 0)[:, 0:rank]
                both = jnp.concatenate([a, a, a, b, b, c], 0).astype(jnp.bfloat16)
                update = jnp.dot(
                    left.T.astype(jnp.bfloat16), both, preferred_element_type=jnp.float32
                )
                work[i, rest:, :] = work[i, rest:, :] - update[rest:]
    if high < rank:
        work[:, high : high + PANEL, 0:rank] = panel
        work[:, high : high + PANEL, rank:] = right


def diagonal_row(columns):
    row = lax.broadcasted_iota(jnp.int32, columns.shape, 0)
    col = lax.broadcasted_iota(jnp.int32, columns.shape, 1)
    return jnp.sum(jnp.where(row == col, columns, 0.0), 0, keepdims=True)


def exchange_kernel(
    blocks,
    nodes,
    count_hbm,
    near_hbm,
    pos_hbm,
    charge_hbm,
    far_hbm,
    proxy_hbm,
    strength_hbm,
    near_out,
    coeffs_out,
    top_gram_ref,
    top_moment_ref,
    win_ref,
    weights,
    targets,
    far_ref,
    count_ref,
    near_ref,
    pos_ref,
    charge_ref,
    proxy_ref,
    strength_ref,
    totals,
    work,
    upper,
    share,
    parts,
    far_sem,
    input_sem,
    win_send,
    win_recv,
    rs_send,
    rs_recv,
    ag_send,
    ag_recv,
):
    block = lax.axis_index("leaf")
    node = lax.axis_index("node")
    slab, y, half = place(node)
    size = pos_ref.shape[1] // 2
    rank = far_ref.shape[1]

    def spatial(ds, dy, core):
        level = slab + ds
        step = (level + 2) // 2 - 1
        level = level - 2 * step
        other = level * 8 + lax.rem(y + dy + ACROSS, ACROSS) * 2 + core
        return (lax.rem(block + step + blocks, blocks), other)

    def in_block(k):
        return (block, lax.rem(node + k, nodes))

    outside = 1 - 2 * slab
    barrier = pltpu.get_barrier_semaphore()
    for k in range(1, nodes):
        pl.semaphore_signal(barrier, inc=1, device_id=in_block(k), device_id_type=MESH)
    for dy in (-1, 0, 1):
        for core in (0, 1):
            target = spatial(-outside, dy, core)
            pl.semaphore_signal(barrier, inc=1, device_id=target, device_id_type=MESH)

    copies = [
        pltpu.make_async_copy(source, target, input_sem.at[i])
        for i, (source, target) in enumerate(
            (
                (pos_hbm, pos_ref),
                (charge_hbm, charge_ref),
                (proxy_hbm, proxy_ref),
                (strength_hbm, strength_ref),
                (near_hbm, near_ref),
                (count_hbm, count_ref),
            )
        )
    ]
    for copy in copies:
        copy.start()
    far_copies = []
    for t in range(2):
        lanes = pl.ds(t * size, size)
        far_copies.append(
            pltpu.make_async_copy(far_hbm.at[lanes], far_ref.at[lanes], far_sem.at[t])
        )
        far_copies[t].start()

    for copy in copies:
        copy.wait()
    for t in range(2):
        lanes = slice(t * size, (t + 1) * size)
        win_ref[4, t, 0:3, :] = pos_ref[:, lanes]
        win_ref[4, t, 3:4, :] = charge_ref[:, lanes]
    centre = centre_of(block, node)
    for t in range(2):
        lanes = slice(t * size, (t + 1) * size)
        targets[t] = target_features(centred(pos_ref[:, lanes], centre))
        distance = jnp.dot(
            targets[t],
            source_features(centred(proxy_ref[:, t, :], centre)),
            preferred_element_type=jnp.float32,
        )
        far_copies[t].wait()
        response = far_ref[lanes, :] + lax.rsqrt(distance) * strength_ref[t : t + 1, :]
        gram = lax.dot_general(
            response,
            response,
            (((0,), (0,)), ((), ())),
            precision=HIGHEST,
            preferred_element_type=jnp.float32,
        )
        moment = jnp.dot(
            jnp.broadcast_to(charge_ref[:, lanes], (8, size)),
            response,
            precision=HIGHEST,
            preferred_element_type=jnp.float32,
        )[0:1]
        work[t, :, 0:rank] = gram
        total = gram if t == 0 else total + gram
        total_moment = moment if t == 0 else total_moment + moment
        work[t, :, rank:] = jnp.broadcast_to(moment, (rank, rank)).T
    rows = rank // nodes
    for n in range(nodes):
        share[n, 0:rows, :] = total[n * rows : (n + 1) * rows]
        share[n, rows : rows + 1, :] = total_moment

    pl.semaphore_wait(barrier, nodes - 1 + 6)

    rs = []
    for k in range(1, nodes):
        target = in_block(k)
        rs.append(
            pltpu.make_async_remote_copy(
                src_ref=share.at[target[1]],
                dst_ref=parts.at[node],
                send_sem=rs_send.at[k],
                recv_sem=rs_recv.at[k],
                device_id=target,
                device_id_type=MESH,
            )
        )
        rs[-1].start()
    window = {}
    for ds in (-1, 1, 0):
        for dy in (-1, 0, 1):
            slot = 4 + 3 * ds + dy
            if slot != 4:
                window[8 - slot] = pltpu.make_async_remote_copy(
                    src_ref=win_ref.at[4, pl.ds(0, 2)],
                    dst_ref=win_ref.at[8 - slot, pl.ds(0, 2)],
                    send_sem=win_send.at[8 - slot],
                    recv_sem=win_recv.at[8 - slot],
                    device_id=spatial(ds, dy, half),
                    device_id_type=MESH,
                )
                window[8 - slot].start()

    forwards = {}

    def forward(slot):
        forwards[slot] = pltpu.make_async_remote_copy(
            src_ref=win_ref.at[slot, pl.ds(1 - half, 1)],
            dst_ref=win_ref.at[slot, pl.ds(2, 1)],
            send_sem=win_send.at[9 + slot],
            recv_sem=win_recv.at[9 + slot],
            device_id=(block, node + 1 - 2 * half),
            device_id_type=MESH,
        )
        forwards[slot].start()

    forward(4)
    parts[node] = share[node]

    read_weights(block, node, near_ref, count_ref, weights)
    totals[...] = jnp.zeros_like(totals)

    def near(sources):
        return near_work(sources, half, centre, win_ref, weights, targets, totals)

    panels = range(rank // PANEL)
    factorize(work, upper, panels[:EARLY], near([(4, 0), (4, 1)]), 4 * (size // PIECE))

    for copy in rs:
        copy.wait_recv()
    sums = parts[0]
    for n in range(1, nodes):
        sums = sums + parts[n]
    top_gram_ref[node] = sums[0:rows]
    top_moment_ref[...] = sums[rows : rows + 1]
    ag = []
    for k in range(1, nodes):
        ag.append(
            pltpu.make_async_remote_copy(
                src_ref=top_gram_ref.at[node],
                dst_ref=top_gram_ref.at[node],
                send_sem=ag_send.at[k],
                recv_sem=ag_recv.at[k],
                device_id=in_block(k),
                device_id_type=MESH,
            )
        )
        ag[-1].start()

    late = (4,)
    for group in GROUPS:
        for slot in group:
            window[slot].wait_recv()
            forward(slot)
        for slot in late:
            forwards[slot].wait_recv()
        sources = [(slot, 2) for slot in late]
        sources += [(slot, w) for slot in group for w in range(2)]
        sources = [source for source in sources if source not in LATE]
        work_left = near(sources)
        if group == GROUPS[0]:
            tiles = len(late) + 4 * len(group)
            factorize(work, upper, panels[EARLY:], work_left, tiles * (size // PIECE))
            for i in range(2):
                coeffs_out[i : i + 1, :] = diagonal_row(upper[i, :, rank:])
        for _ in work_left:
            pass
        late = group
    for slot in late:
        forwards[slot].wait_recv()
    for _ in near([(slot, 2) for slot in late if (slot, 2) not in LATE]):
        pass
    for t in range(2):
        near_out[:, t * size : (t + 1) * size] = lane_sums(totals[t])
    for copy in rs + list(window.values()) + list(forwards.values()):
        copy.wait_send()
    for copy in ag:
        copy.wait()


def top_kernel(
    near_ref,
    coeffs_ref,
    gram_ref,
    moment_ref,
    win_ref,
    weights,
    targets,
    near_out,
    coeffs_out,
    factor_out,
    top_coeffs_out,
    totals,
    work,
    upper,
):
    block = lax.axis_index("leaf")
    node = lax.axis_index("node")
    half = place(node)[2]
    rank = work.shape[1]
    size = win_ref.shape[3]
    totals[...] = jnp.zeros_like(totals)
    near = near_work(LATE, half, centre_of(block, node), win_ref, weights, targets, totals)
    pieces = sum(2 if w < 2 else 1 for _, w in LATE) * (size // PIECE)
    coeffs_out[...] = coeffs_ref[...]
    work[0, :, 0:rank] = gram_ref[...].reshape(rank, rank)
    work[0, :, rank:] = jnp.broadcast_to(moment_ref[...], (rank, rank)).T
    factorize(work, upper, range(rank // PANEL), near, pieces)
    for t in range(2):
        lanes = slice(t * size, (t + 1) * size)
        near_out[:, lanes] = near_ref[:, lanes] + lane_sums(totals[t])
    work[0, :, 0:rank] = upper[0, :, 0:rank].T
    rows = factor_out.shape[1]
    mine = pl.ds(pl.multiple_of(node * rows, rows), rows)
    factor_out[0] = work[0, mine, 0:rank]
    top_coeffs_out[...] = diagonal_row(upper[0, mine, rank:])[:, 0:rows]


def body(positions, charges, near_list, near_count, far_sample, proxies, strengths):
    blocks = lax.axis_size("leaf")
    nodes = lax.axis_size("node")
    size = charges.shape[0] // near_count.shape[0]
    rank = far_sample.shape[1]
    rows = rank // nodes
    vmem = pl.BlockSpec(memory_space=pltpu.VMEM)
    shape = lambda *dims: jax.ShapeDtypeStruct(dims, jnp.float32)
    scratch = lambda *dims: pltpu.VMEM(dims, jnp.float32)
    semaphores = lambda n: pltpu.SemaphoreType.DMA((n,))
    parts = pl.pallas_call(
        functools.partial(exchange_kernel, blocks, nodes),
        out_shape=(
            scratch(1, 2 * size),
            scratch(2, rank),
            scratch(nodes, rows, rank),
            scratch(1, rank),
            scratch(9, 3, 4, size),
            scratch(2, 32, 128),
            pltpu.VMEM((2, size, 64), jnp.bfloat16),
        ),
        in_specs=[pl.BlockSpec(memory_space=pl.ANY)] * 7,
        out_specs=(vmem,) * 7,
        scratch_shapes=[
            scratch(2 * size, rank),
            pltpu.VMEM((1, 2), jnp.int32),
            pltpu.VMEM(near_list.shape, jnp.int32),
            scratch(3, 2 * size),
            scratch(1, 2 * size),
            scratch(3, 2, rank),
            scratch(2, rank),
            scratch(2, size, 128),
            scratch(2, rank, 2 * rank),
            scratch(2, rank, 2 * rank),
            scratch(nodes, rows + 1, rank),
            scratch(nodes, rows + 1, rank),
            semaphores(2),
            semaphores(6),
            semaphores(18),
            semaphores(18),
            semaphores(nodes),
            semaphores(nodes),
            semaphores(nodes),
            semaphores(nodes),
        ],
        compiler_params=pltpu.CompilerParams(collective_id=0, has_side_effects=True),
        name="exchange",
    )(
        near_count[None, :],
        near_list,
        positions,
        charges[None, :],
        far_sample,
        jnp.transpose(proxies, (1, 0, 2)),
        strengths,
    )
    near, coeffs, factor, top_coeffs = pl.pallas_call(
        top_kernel,
        out_shape=(shape(1, 2 * size), shape(2, rank), shape(1, rows, rank), shape(1, rows)),
        in_specs=[vmem] * 7,
        out_specs=(vmem,) * 4,
        scratch_shapes=[
            scratch(2, size, 128),
            scratch(1, rank, 2 * rank),
            scratch(1, rank, 2 * rank),
        ],
        name="top",
    )(*(pltpu.with_memory_space_constraint(part, pltpu.VMEM) for part in parts))
    return (near.reshape(-1), coeffs, factor, top_coeffs)


def solution(mesh):
    in_specs = (
        P(None, ("leaf", "node")),
        P(("leaf", "node")),
        P(("leaf", "node"), None),
        P(("leaf", "node")),
        P(("leaf", "node"), None),
        P(("leaf", "node"), None, None),
        P(("leaf", "node"), None),
    )
    out_specs = (
        P(("leaf", "node")),
        P(("leaf", "node"), None),
        P("leaf", "node", None),
        P("leaf", "node"),
    )
    return jax.shard_map(body, mesh=mesh, in_specs=in_specs, out_specs=out_specs, check_vma=False)
```

```python
import functools

import jax
import jax.numpy as jnp
from jax import lax
from jax.experimental import pallas as pl
from jax.experimental.pallas import tpu as pltpu
from jax.sharding import PartitionSpec as P

soft_square = 0.0025
ACROSS = 4
PANEL = 16
PIECE = 128
MESH = pl.DeviceIdType.MESH
HIGHEST = lax.Precision.HIGHEST
LATE = ((8, 0), (8, 1), (8, 2))
EARLY = 7
GROUPS = ((3, 5), (0, 1, 2), (6, 7, 8))


def split3(v):
    high = v.astype(jnp.bfloat16).astype(jnp.float32)
    rest = v - high
    mid = rest.astype(jnp.bfloat16).astype(jnp.float32)
    return high, mid, rest - mid


def feature_rows(xyz, fourth, fifth):
    row = lax.broadcasted_iota(jnp.int32, (8, xyz.shape[1]), 0)
    rows = jnp.where(row == 4, fifth, 0.0)
    rows = jnp.where(row == 3, fourth, rows)
    for k in range(3):
        rows = jnp.where(row == k, xyz[k : k + 1], rows)
    return split3(rows)


def source_features(xyz):
    high, mid, low = feature_rows(xyz, jnp.sum(xyz * xyz, 0, keepdims=True), 1.0)
    return jnp.concatenate([high, high, high, mid, mid, mid, low, low], 0).astype(jnp.bfloat16)


def target_features(xyz):
    norm = jnp.sum(xyz * xyz, 0, keepdims=True) + soft_square
    high, mid, low = feature_rows(-2.0 * xyz, 1.0, norm)
    return jnp.concatenate([high, mid, low, high, mid, low, high, mid], 0).T.astype(jnp.bfloat16)


def place(node):
    return node // 8, lax.rem(node // 2, ACROSS), lax.rem(node, 2)


def centre_of(block, node):
    slab, y, half = place(node)
    return (
        (2 * block + slab).astype(jnp.float32) + 0.5,
        y.astype(jnp.float32) + 0.5,
        (2 * half).astype(jnp.float32) + 1.0,
    )


def centred(rows, centre):
    row = lax.broadcasted_iota(jnp.int32, rows.shape, 0)
    shift = jnp.where(row == 0, centre[0], jnp.where(row == 1, centre[1], centre[2]))
    return rows - shift


def read_weights(block, node, near_ref, count_ref, weights):
    slab, y, half = place(node)
    row = lax.broadcasted_iota(jnp.int32, (32, near_ref.shape[1]), 0)
    lane = lax.broadcasted_iota(jnp.int32, (32, near_ref.shape[1]), 1)
    ids = jnp.full(row.shape, -1, jnp.int32)
    for k in range(27):
        ds, dy, w = k // 9 - 1, k // 3 % 3 - 1, k % 3
        z = 2 * half + w if w < 2 else 2 - half
        base = (2 * block + slab + ds) * ACROSS * ACROSS
        leaf = base + lax.rem(y + dy + ACROSS, ACROSS) * ACROSS + z
        ids = jnp.where(row == k, leaf, ids)
    for t in range(2):
        hit = (near_ref[t : t + 1, :] == ids) & (lane < count_ref[0:1, t : t + 1])
        weight = jnp.sum(jnp.where(hit, 1.0, 0.0), 1, keepdims=True)
        own = row[:, 0:1] == 12 + t
        weights[t] = jnp.broadcast_to(jnp.where(own, 1.0, weight), (32, 128))


def near_work(sources, half, centre, win_ref, weights, targets, totals):
    size = win_ref.shape[3]

    def piece(t, rows, features, charges):
        distance = jnp.dot(targets[t, rows, :], features, preferred_element_type=jnp.float32)
        terms = lax.rsqrt(distance) * charges
        total = terms[:, 0:128]
        for k in range(1, size // 128):
            total = total + terms[:, k * 128 : (k + 1) * 128]
        totals[t, rows, :] += total

    for slot, w in sources:
        points = win_ref[slot, w]
        features = source_features(centred(points[0:3], centre))
        for t in (0, 1) if w < 2 else (1 - half,):
            weight = weights[t, slot * 3 + w : slot * 3 + w + 1, :]
            charges = points[3:4] * jnp.concatenate([weight] * (size // 128), 1)
            for start in range(0, size, PIECE):
                piece(t, slice(start, start + PIECE), features, charges)
                yield


def lane_sums(totals):
    ones = jnp.ones((8, totals.shape[1]), jnp.float32)
    return lax.dot_general(
        ones, totals, (((1,), (1,)), ((), ())), precision=HIGHEST, preferred_element_type=jnp.float32
    )[0:1]


def factorize(work, upper, panels, other=(), pieces=0):
    other = iter(other)
    pivots = len(panels) * PANEL
    steps = 0
    count, rank = work.shape[0], work.shape[1]
    row = lax.broadcasted_iota(jnp.int32, (count, PANEL, rank), 1)
    col = lax.broadcasted_iota(jnp.int32, (count, PANEL, rank), 2)

    def spread(rows, low):
        return [
            jnp.broadcast_to(rows[:, :, low + j : low + j + 1], (count, PANEL, rank))
            for j in range(PANEL)
        ]

    low = panels[0] * PANEL
    panel = work[:, low : low + PANEL, 0:rank]
    right = work[:, low : low + PANEL, rank:]
    for low in (p * PANEL for p in panels):
        high = low + PANEL
        columns = spread(panel, low)
        if high < rank:
            after = work[:, high : high + PANEL, 0:rank]
            after_right = work[:, high : high + PANEL, rank:]
            after_columns = spread(after, low)
        done = jnp.zeros((count, PANEL, rank), jnp.float32)
        done_right = done
        for j in range(PANEL):
            for _ in range(pieces * steps // pivots, pieces * (steps + 1) // pivots):
                next(other)
            steps += 1
            inverse = lax.rsqrt(columns[j][:, j : j + 1, :])
            below = jnp.where(row > j, columns[j] * inverse, 0.0)
            pivot = panel[:, j : j + 1] * inverse
            pivot_right = right[:, j : j + 1] * inverse
            done = jnp.where(row == j, pivot, done)
            done_right = jnp.where(row == j, pivot_right, done_right)
            scaled = [columns[k][:, j : j + 1, :] * inverse for k in range(j + 1, PANEL)]
            if j + 1 < PANEL:
                panel = panel - below * pivot
                right = right - below * pivot_right
                for k in range(j + 1, PANEL):
                    columns[k] = columns[k] - below * scaled[k - j - 1]
            if high < rank:
                further = after_columns[j] * inverse
                after = after - further * pivot
                after_right = after_right - further * pivot_right
                for k in range(j + 1, PANEL):
                    after_columns[k] = after_columns[k] - further * scaled[k - j - 1]
        done = jnp.where(col >= row + low, done, 0.0)
        upper[:, low:high, 0:rank] = done
        upper[:, low:high, rank:] = done_right
        if high < rank:
            panel, right = after, after_right
        rest = high + PANEL
        if rest < rank:
            for i in range(count):
                a, b, c = split3(jnp.concatenate([done[i], done_right[i]], 1))
                left = jnp.concatenate([a, b, c, a, b, a], 0)[:, 0:rank]
                both = jnp.concatenate([a, a, a, b, b, c], 0).astype(jnp.bfloat16)
                update = jnp.dot(
                    left.T.astype(jnp.bfloat16), both, preferred_element_type=jnp.float32
                )
                work[i, rest:, :] = work[i, rest:, :] - update[rest:]
    if high < rank:
        work[:, high : high + PANEL, 0:rank] = panel
        work[:, high : high + PANEL, rank:] = right


def diagonal_row(columns):
    row = lax.broadcasted_iota(jnp.int32, columns.shape, 0)
    col = lax.broadcasted_iota(jnp.int32, columns.shape, 1)
    return jnp.sum(jnp.where(row == col, columns, 0.0), 0, keepdims=True)


def exchange_kernel(
    blocks,
    nodes,
    count_hbm,
    near_hbm,
    pos_hbm,
    charge_hbm,
    far_hbm,
    proxy_hbm,
    strength_hbm,
    near_out,
    coeffs_out,
    top_gram_ref,
    top_moment_ref,
    win_ref,
    weights,
    targets,
    far_ref,
    count_ref,
    near_ref,
    pos_ref,
    charge_ref,
    proxy_ref,
    strength_ref,
    totals,
    work,
    upper,
    share,
    parts,
    far_sem,
    input_sem,
    win_send,
    win_recv,
    rs_send,
    rs_recv,
    ag_send,
    ag_recv,
):
    block = lax.axis_index("leaf")
    node = lax.axis_index("node")
    slab, y, half = place(node)
    size = pos_ref.shape[1] // 2
    rank = far_ref.shape[1]

    def spatial(ds, dy, core):
        level = slab + ds
        step = (level + 2) // 2 - 1
        level = level - 2 * step
        other = level * 8 + lax.rem(y + dy + ACROSS, ACROSS) * 2 + core
        return (lax.rem(block + step + blocks, blocks), other)

    def in_block(k):
        return (block, lax.rem(node + k, nodes))

    outside = 1 - 2 * slab
    farthest = sorted(range(1, nodes), key=lambda k: -min(k, nodes - k))
    barrier = pltpu.get_barrier_semaphore()
    for k in farthest:
        pl.semaphore_signal(barrier, inc=1, device_id=in_block(k), device_id_type=MESH)
    for dy in (-1, 0, 1):
        for core in (0, 1):
            target = spatial(-outside, dy, core)
            pl.semaphore_signal(barrier, inc=1, device_id=target, device_id_type=MESH)

    copies = [
        pltpu.make_async_copy(source, target, input_sem.at[i])
        for i, (source, target) in enumerate(
            (
                (pos_hbm, pos_ref),
                (charge_hbm, charge_ref),
                (proxy_hbm, proxy_ref),
                (strength_hbm, strength_ref),
                (near_hbm, near_ref),
                (count_hbm, count_ref),
            )
        )
    ]
    for copy in copies:
        copy.start()
    far_copies = []
    for t in range(2):
        lanes = pl.ds(t * size, size)
        far_copies.append(
            pltpu.make_async_copy(far_hbm.at[lanes], far_ref.at[lanes], far_sem.at[t])
        )
        far_copies[t].start()

    for copy in copies:
        copy.wait()
    for t in range(2):
        lanes = slice(t * size, (t + 1) * size)
        win_ref[4, t, 0:3, :] = pos_ref[:, lanes]
        win_ref[4, t, 3:4, :] = charge_ref[:, lanes]
    centre = centre_of(block, node)
    for t in range(2):
        lanes = slice(t * size, (t + 1) * size)
        targets[t] = target_features(centred(pos_ref[:, lanes], centre))
        distance = jnp.dot(
            targets[t],
            source_features(centred(proxy_ref[:, t, :], centre)),
            preferred_element_type=jnp.float32,
        )
        far_copies[t].wait()
        response = far_ref[lanes, :] + lax.rsqrt(distance) * strength_ref[t : t + 1, :]
        gram = lax.dot_general(
            response,
            response,
            (((0,), (0,)), ((), ())),
            precision=HIGHEST,
            preferred_element_type=jnp.float32,
        )
        moment = jnp.dot(
            jnp.broadcast_to(charge_ref[:, lanes], (8, size)),
            response,
            precision=HIGHEST,
            preferred_element_type=jnp.float32,
        )[0:1]
        work[t, :, 0:rank] = gram
        total = gram if t == 0 else total + gram
        total_moment = moment if t == 0 else total_moment + moment
        work[t, :, rank:] = jnp.broadcast_to(moment, (rank, rank)).T
    rows = rank // nodes
    for n in range(nodes):
        share[n, 0:rows, :] = total[n * rows : (n + 1) * rows]
        share[n, rows : rows + 1, :] = total_moment

    pl.semaphore_wait(barrier, nodes - 1 + 6)

    rs = []
    for k in farthest:
        target = in_block(k)
        rs.append(
            pltpu.make_async_remote_copy(
                src_ref=share.at[target[1]],
                dst_ref=parts.at[node],
                send_sem=rs_send.at[k],
                recv_sem=rs_recv.at[k],
                device_id=target,
                device_id_type=MESH,
            )
        )
        rs[-1].start()
    window = {}
    for ds in (-1, 1, 0):
        for dy in (-1, 0, 1):
            slot = 4 + 3 * ds + dy
            if slot != 4:
                window[8 - slot] = pltpu.make_async_remote_copy(
                    src_ref=win_ref.at[4, pl.ds(0, 2)],
                    dst_ref=win_ref.at[8 - slot, pl.ds(0, 2)],
                    send_sem=win_send.at[8 - slot],
                    recv_sem=win_recv.at[8 - slot],
                    device_id=spatial(ds, dy, half),
                    device_id_type=MESH,
                )
                window[8 - slot].start()

    forwards = {}

    def forward(slot):
        forwards[slot] = pltpu.make_async_remote_copy(
            src_ref=win_ref.at[slot, pl.ds(1 - half, 1)],
            dst_ref=win_ref.at[slot, pl.ds(2, 1)],
            send_sem=win_send.at[9 + slot],
            recv_sem=win_recv.at[9 + slot],
            device_id=(block, node + 1 - 2 * half),
            device_id_type=MESH,
        )
        forwards[slot].start()

    forward(4)
    parts[node] = share[node]

    read_weights(block, node, near_ref, count_ref, weights)
    totals[...] = jnp.zeros_like(totals)

    def near(sources):
        return near_work(sources, half, centre, win_ref, weights, targets, totals)

    panels = range(rank // PANEL)
    factorize(work, upper, panels[:EARLY], near([(4, 0), (4, 1)]), 4 * (size // PIECE))

    for copy in rs:
        copy.wait_recv()
    sums = parts[0]
    for n in range(1, nodes):
        sums = sums + parts[n]
    top_gram_ref[node] = sums[0:rows]
    top_moment_ref[...] = sums[rows : rows + 1]
    ag = []
    for k in farthest:
        ag.append(
            pltpu.make_async_remote_copy(
                src_ref=top_gram_ref.at[node],
                dst_ref=top_gram_ref.at[node],
                send_sem=ag_send.at[k],
                recv_sem=ag_recv.at[k],
                device_id=in_block(k),
                device_id_type=MESH,
            )
        )
        ag[-1].start()

    late = (4,)
    for group in GROUPS:
        for slot in group:
            window[slot].wait_recv()
            forward(slot)
        for slot in late:
            forwards[slot].wait_recv()
        sources = [(slot, 2) for slot in late]
        sources += [(slot, w) for slot in group for w in range(2)]
        sources = [source for source in sources if source not in LATE]
        work_left = near(sources)
        if group == GROUPS[0]:
            tiles = len(late) + 4 * len(group)
            factorize(work, upper, panels[EARLY:], work_left, tiles * (size // PIECE))
            for i in range(2):
                coeffs_out[i : i + 1, :] = diagonal_row(upper[i, :, rank:])
        for _ in work_left:
            pass
        late = group
    for slot in late:
        forwards[slot].wait_recv()
    for _ in near([(slot, 2) for slot in late if (slot, 2) not in LATE]):
        pass
    for t in range(2):
        near_out[:, t * size : (t + 1) * size] = lane_sums(totals[t])
    for copy in rs + list(window.values()) + list(forwards.values()):
        copy.wait_send()
    for copy in ag:
        copy.wait()


def top_kernel(
    near_ref,
    coeffs_ref,
    gram_ref,
    moment_ref,
    win_ref,
    weights,
    targets,
    near_out,
    coeffs_out,
    factor_out,
    top_coeffs_out,
    totals,
    work,
    upper,
):
    block = lax.axis_index("leaf")
    node = lax.axis_index("node")
    half = place(node)[2]
    rank = work.shape[1]
    size = win_ref.shape[3]
    totals[...] = jnp.zeros_like(totals)
    near = near_work(LATE, half, centre_of(block, node), win_ref, weights, targets, totals)
    pieces = sum(2 if w < 2 else 1 for _, w in LATE) * (size // PIECE)
    coeffs_out[...] = coeffs_ref[...]
    work[0, :, 0:rank] = gram_ref[...].reshape(rank, rank)
    work[0, :, rank:] = jnp.broadcast_to(moment_ref[...], (rank, rank)).T
    factorize(work, upper, range(rank // PANEL), near, pieces)
    for t in range(2):
        lanes = slice(t * size, (t + 1) * size)
        near_out[:, lanes] = near_ref[:, lanes] + lane_sums(totals[t])
    work[0, :, 0:rank] = upper[0, :, 0:rank].T
    rows = factor_out.shape[1]
    mine = pl.ds(pl.multiple_of(node * rows, rows), rows)
    factor_out[0] = work[0, mine, 0:rank]
    top_coeffs_out[...] = diagonal_row(upper[0, mine, rank:])[:, 0:rows]


def body(positions, charges, near_list, near_count, far_sample, proxies, strengths):
    blocks = lax.axis_size("leaf")
    nodes = lax.axis_size("node")
    size = charges.shape[0] // near_count.shape[0]
    rank = far_sample.shape[1]
    rows = rank // nodes
    vmem = pl.BlockSpec(memory_space=pltpu.VMEM)
    shape = lambda *dims: jax.ShapeDtypeStruct(dims, jnp.float32)
    scratch = lambda *dims: pltpu.VMEM(dims, jnp.float32)
    semaphores = lambda n: pltpu.SemaphoreType.DMA((n,))
    parts = pl.pallas_call(
        functools.partial(exchange_kernel, blocks, nodes),
        out_shape=(
            scratch(1, 2 * size),
            scratch(2, rank),
            scratch(nodes, rows, rank),
            scratch(1, rank),
            scratch(9, 3, 4, size),
            scratch(2, 32, 128),
            pltpu.VMEM((2, size, 64), jnp.bfloat16),
        ),
        in_specs=[pl.BlockSpec(memory_space=pl.ANY)] * 7,
        out_specs=(vmem,) * 7,
        scratch_shapes=[
            scratch(2 * size, rank),
            pltpu.VMEM((1, 2), jnp.int32),
            pltpu.VMEM(near_list.shape, jnp.int32),
            scratch(3, 2 * size),
            scratch(1, 2 * size),
            scratch(3, 2, rank),
            scratch(2, rank),
            scratch(2, size, 128),
            scratch(2, rank, 2 * rank),
            scratch(2, rank, 2 * rank),
            scratch(nodes, rows + 1, rank),
            scratch(nodes, rows + 1, rank),
            semaphores(2),
            semaphores(6),
            semaphores(18),
            semaphores(18),
            semaphores(nodes),
            semaphores(nodes),
            semaphores(nodes),
            semaphores(nodes),
        ],
        compiler_params=pltpu.CompilerParams(collective_id=0, has_side_effects=True),
        name="exchange",
    )(
        near_count[None, :],
        near_list,
        positions,
        charges[None, :],
        far_sample,
        jnp.transpose(proxies, (1, 0, 2)),
        strengths,
    )
    near, coeffs, factor, top_coeffs = pl.pallas_call(
        top_kernel,
        out_shape=(shape(1, 2 * size), shape(2, rank), shape(1, rows, rank), shape(1, rows)),
        in_specs=[vmem] * 7,
        out_specs=(vmem,) * 4,
        scratch_shapes=[
            scratch(2, size, 128),
            scratch(1, rank, 2 * rank),
            scratch(1, rank, 2 * rank),
        ],
        name="top",
    )(*(pltpu.with_memory_space_constraint(part, pltpu.VMEM) for part in parts))
    return (near.reshape(-1), coeffs, factor, top_coeffs)


def solution(mesh):
    in_specs = (
        P(None, ("leaf", "node")),
        P(("leaf", "node")),
        P(("leaf", "node"), None),
        P(("leaf", "node")),
        P(("leaf", "node"), None),
        P(("leaf", "node"), None, None),
        P(("leaf", "node"), None),
    )
    out_specs = (
        P(("leaf", "node")),
        P(("leaf", "node"), None),
        P("leaf", "node", None),
        P("leaf", "node"),
    )
    return jax.shard_map(body, mesh=mesh, in_specs=in_specs, out_specs=out_specs, check_vma=False)
```
